32 devices in a mesh: clip: 2 (over core), frame: 16 (over z, y, x).
Axes of the slice: x: 2, y: 2, z: 4, core: 2. Of those that a mesh axis runs over, the one named last changes fastest.
Arguments:
- hidden: bfloat16 [2, 16, 128, 1664], P('clip', 'frame'), may hold values from -6 to 6
- queries: bfloat16 [2, 16, 128, 832], P('clip', 'frame'), may hold values from -8 to 8
- keys: bfloat16 [2, 16, 128, 832], P('clip', 'frame'), may hold values from -8 to 8
- values: bfloat16 [2, 16, 128, 832], P('clip', 'frame'), may hold values from -6 to 6
- grad_attn: bfloat16 [2, 16, 128, 832], P('clip', 'frame'), may hold values from -6 to 6
- w_qkv: bfloat16 [1664, 2496], P('frame'), may hold values from -0.15625 to 0.15625
Outputs:
- grad_hidden: bfloat16 [2, 16, 128, 1664], P('clip', 'frame')
- grad_w: float32 [1664, 832], P('frame')
The draws below stay inside these ranges and needn't reach their ends.
All inputs are finite; a program needn't handle non-finite values.
Results may differ from the reference program's by a relative error of at most 0.0059.
Values may be sent and summed in bfloat16 or wider, within the bound.
A program may use at most 64 MiB of HBM per device.

```python
import math
import jax
import jax.numpy as jnp
from jax import lax

D = 1664
HDIM = 104
HEADS = 8
P_SIZE = 128
HD = 832
FRAMES = 16
CLIPS = 2


def drawn_pair(key):
    base_key = jax.random.fold_in(key, 11)
    key_query, key_keys = jax.random.split(base_key, 2)
    array_shape = (CLIPS, FRAMES, P_SIZE, HEADS * HDIM)
    query_draw = jnp.clip(jax.random.normal(key_query, array_shape, jnp.float32), -4.0, 4.0)
    key_draw = jnp.clip(jax.random.normal(key_keys, array_shape, jnp.float32), -4.0, 4.0)
    return (query_draw, key_draw)


def draw_queries(key, part):
    query_draw, key_draw = drawn_pair(key)
    return query_draw.astype(jnp.bfloat16)


def draw_keys(key, part):
    query_draw, key_draw = drawn_pair(key)
    return key_draw.astype(jnp.bfloat16)


def with_spikes(values, stream_key, source, target, blocks, factor):
    owner, partner = [(jnp.arange(values.shape[axis_at]) // (values.shape[axis_at] // blocks)).reshape([-1 if axis == axis_at else 1 for axis in range(values.ndim)]) for axis_at in (source, target)]
    chosen = jax.random.permutation(stream_key, blocks)[partner]
    strong = (owner == chosen) | (owner == (partner + blocks // 2) % blocks)
    return jnp.where(strong, factor * values, values)


def block_scale(stream_key, dims, pieces, low, top_value):
    factor_of = 1.0
    for position, blocks in pieces:
        draws = jax.random.uniform(jax.random.fold_in(jax.random.fold_in(stream_key, 6), position), (blocks,), jnp.float32, low / len(pieces), top_value / len(pieces))
        factor_of = factor_of * jnp.repeat(jnp.exp(draws), dims[position] // blocks).reshape((-1,) + (1,) * (len(dims) - 1 - position))
    return factor_of


def centred(stream_key, dims, deviation, limit, cuts=(), kind=jnp.bfloat16):
    drawn = jax.random.normal(stream_key, dims, jnp.float32) * deviation
    if len(cuts) > 0:
        drawn = block_scale(stream_key, dims, cuts, -0.22, 0.18) * drawn
    return jnp.clip(drawn, min=-limit, max=limit).astype(kind)


def noise_with(stream_key, shape, deviation, reach, cuts, heavy, kind=jnp.bfloat16):
    result = deviation * jax.random.normal(stream_key, shape, jnp.float32)
    if cuts:
        result = result * block_scale(stream_key, shape, cuts, -0.22, 0.18)
    return jnp.clip(with_spikes(result, jax.random.fold_in(stream_key, 3), *heavy), -reach, reach).astype(kind)


def setup_inputs(seed: int = 0) -> dict:
    seeds = jax.random.split(jax.random.key(seed), 7)
    hidden = noise_with(seeds[0], (CLIPS, FRAMES, P_SIZE, D), 1.0, 6.0, ((0, 2), (1, 16)), (1, 3, 16, 2.0))
    queries = draw_queries(jax.random.fold_in(seeds[6], 71), 0)
    keys = draw_keys(jax.random.fold_in(seeds[6], 71), 0)
    values = centred(seeds[3], (CLIPS, FRAMES, P_SIZE, HD), 1.0, 6.0, ((0, 2), (1, 16)))
    grad_attn = centred(seeds[4], (CLIPS, FRAMES, P_SIZE, HD), 1.0, 6.0, ((0, 2), (1, 16)))
    w_qkv = centred(seeds[5], (D, 3 * HD), D ** -0.5, 0.15625, ((0, 16),))
    return {"hidden": hidden, "queries": queries, "keys": keys, "values": values, "grad_attn": grad_attn, "w_qkv": w_qkv}


def attend_back(queries, keys, values, grad_out):
    score_scale = 1.0 / math.sqrt(HDIM)
    q_full = queries.astype(jnp.float32)
    k_full = keys.astype(jnp.float32)
    v_full = values.astype(jnp.float32)
    g_full = grad_out.astype(jnp.float32)
    scores = jnp.einsum('fpnd,gpnd->pnfg', q_full, k_full) * score_scale
    attn_probs = jax.nn.softmax(scores, axis=-1)
    probs_bf = lax.optimization_barrier(attn_probs.astype(jnp.bfloat16)).astype(jnp.float32)
    grad_v = jnp.einsum('pnfg,fpnd->gpnd', probs_bf, g_full).astype(jnp.bfloat16)
    grad_probs = jnp.einsum('fpnd,gpnd->pnfg', g_full, v_full)
    grad_scores = attn_probs * (grad_probs - lax.optimization_barrier(jnp.sum(attn_probs * grad_probs, axis=-1, keepdims=True)))
    scores_bf = lax.optimization_barrier(grad_scores.astype(jnp.bfloat16)).astype(jnp.float32)
    grad_q = (jnp.einsum('pnfg,gpnd->fpnd', scores_bf, k_full) * score_scale).astype(jnp.bfloat16)
    grad_k = (jnp.einsum('pnfg,fpnd->gpnd', scores_bf, q_full) * score_scale).astype(jnp.bfloat16)
    return (grad_q, grad_k, grad_v)

def to_heads(tensor):
    return tensor.reshape(FRAMES, P_SIZE, HEADS, HDIM)

def reference(hidden, queries, keys, values, grad_attn, w_qkv):
    row_count = FRAMES * P_SIZE
    inner_width = HEADS * HDIM

    def one_clip(running, inputs):
        hid_clip, q_clip, k_clip, v_clip, g_clip = inputs
        grad_q, grad_k, grad_v = attend_back(to_heads(q_clip), to_heads(k_clip), to_heads(v_clip), to_heads(g_clip))
        value_rows = grad_v.reshape(row_count, inner_width)
        grad_cat = jnp.concatenate([grad_q.reshape(row_count, inner_width), grad_k.reshape(row_count, inner_width), value_rows], axis=1)
        grad_hid = jnp.dot(grad_cat, w_qkv.T, preferred_element_type=jnp.float32).astype(jnp.bfloat16)
        hidden_rows = hid_clip.reshape(row_count, D)
        running = running + jnp.dot(hidden_rows.T, value_rows, preferred_element_type=jnp.float32)
        return (running, grad_hid.reshape(FRAMES, P_SIZE, D))
    start_grad = jnp.zeros((D, inner_width), jnp.float32)
    running, grad_hidden = lax.scan(one_clip, start_grad, (hidden, queries, keys, values, grad_attn))
    return (grad_hidden, running / CLIPS)
```

```python
import functools
import math

import jax
import jax.numpy as jnp
from jax import lax
from jax.experimental import pallas as pl
from jax.experimental.pallas import tpu as pltpu
from jax.sharding import PartitionSpec as P

HDIM = 104


def attend_back(queries, keys, values, grad_out):
    score_scale = 1.0 / math.sqrt(HDIM)
    scores = (
        jnp.einsum("fpnd,gpnd->pnfg", queries, keys, preferred_element_type=jnp.float32)
        * score_scale
    )
    attn_probs = jax.nn.softmax(scores, axis=-1)
    probs_bf = attn_probs.astype(jnp.bfloat16)
    grad_v = jnp.einsum(
        "pnfg,fpnd->gpnd", probs_bf, grad_out, preferred_element_type=jnp.float32
    ).astype(jnp.bfloat16)
    grad_probs = jnp.einsum("fpnd,gpnd->pnfg", grad_out, values, preferred_element_type=jnp.float32)
    grad_scores = attn_probs * (
        grad_probs - jnp.sum(attn_probs * grad_probs, axis=-1, keepdims=True)
    )
    scores_bf = grad_scores.astype(jnp.bfloat16)
    grad_q = (
        jnp.einsum("pnfg,gpnd->fpnd", scores_bf, keys, preferred_element_type=jnp.float32)
        * score_scale
    ).astype(jnp.bfloat16)
    grad_k = (
        jnp.einsum("pnfg,fpnd->gpnd", scores_bf, queries, preferred_element_type=jnp.float32)
        * score_scale
    ).astype(jnp.bfloat16)
    return (grad_q, grad_k, grad_v)


def per_device(hidden, queries, keys, values, grad_attn, w_qkv):
    frames_local = hidden.shape[1]
    patches = hidden.shape[2]
    model_width = hidden.shape[3]
    inner_width = queries.shape[3]
    head_count = inner_width // HDIM
    row_count = frames_local * patches
    head_shape = (frames_local, patches, head_count, HDIM)
    q_local = queries.reshape(head_shape)
    k_local = keys.reshape(head_shape)
    v_local = values.reshape(head_shape)
    g_local = grad_attn.reshape(head_shape)
    q_patch, k_patch, v_patch, g_patch = (
        lax.all_to_all(q_local, "frame", split_axis=1, concat_axis=0, tiled=True),
        lax.all_to_all(k_local, "frame", split_axis=1, concat_axis=0, tiled=True),
        lax.all_to_all(v_local, "frame", split_axis=1, concat_axis=0, tiled=True),
        lax.all_to_all(g_local, "frame", split_axis=1, concat_axis=0, tiled=True),
    )
    grad_q, grad_k, grad_v = attend_back(q_patch, k_patch, v_patch, g_patch)
    grad_q, grad_k, grad_v = (
        lax.all_to_all(grad_q, "frame", split_axis=0, concat_axis=1, tiled=True),
        lax.all_to_all(grad_k, "frame", split_axis=0, concat_axis=1, tiled=True),
        lax.all_to_all(grad_v, "frame", split_axis=0, concat_axis=1, tiled=True),
    )
    value_rows = grad_v.reshape(row_count, inner_width)
    grad_cat = jnp.concatenate(
        [
            grad_q.reshape(row_count, inner_width),
            grad_k.reshape(row_count, inner_width),
            value_rows,
        ],
        axis=1,
    )
    grad_hid = lax.dot_general(
        grad_cat,
        lax.all_gather(w_qkv, "frame", axis=0, tiled=True),
        (((1,), (1,)), ((), ())),
        preferred_element_type=jnp.float32,
    )
    grad_hidden = grad_hid.astype(jnp.bfloat16).reshape(hidden.shape)
    hidden_rows = hidden.reshape(row_count, model_width)
    clip_count = lax.axis_size("clip")
    partial_grad = lax.psum_scatter(
        lax.dot_general(
            hidden_rows, value_rows, (((0,), (0,)), ((), ())), preferred_element_type=jnp.float32
        ),
        "frame",
        scatter_dimension=0,
        tiled=True,
    )
    grad_total = lax.psum(partial_grad, "clip")
    return (grad_hidden, grad_total / clip_count)


AX = {"z": (4, 4), "y": (2, 2), "x": (2, 1)}
N_FRAME = 16
ORDER = (
    "y0", "hop1", "hidden", "spread", "attend_v", "attend_qk", "swap", "hop2", "share", "hop3", "weight",
    "ys", "project", "sum_y", "sum_z", "finish", "collect",
)
CHUNKS = ((0, 256), (256, 512), (512, 832))
COLS = ((0, 384), (384, 832))
W_COLS = ((0, 1280), (1280, 2496))


def move(f, axis, k):
    size, stride = AX[axis]
    digit = lax.rem(lax.div(f, stride), size)
    return f + (lax.rem(digit + k, size) - digit) * stride


def kernel(
    q_hbm, k_hbm, v_hbm, g_hbm, h_hbm, w_hbm,
    gh_ref, gw_ref,
    tq, tk, tv, tg, sq, sk, sv, sg, qb, kb, vb, gb,
    hb, hs, hall, w0, w1, acc_q, acc_k, acc_v, out_v, gall, cat, ob, land,
    dws, y_s, y_r, z_s, z_r, fin_s, fin_r,
    loc, t_sem, a_send, a_recv, b_send, b_recv, wy_send, wy_recv, wz_send, wz_recv, wc_send, wc_recv,
    h_send, h_recv, x_sem, g_send, g_recv, o_send, o_recv, ry_sem, rz_send, rz_recv, f_sem,
):
    c = lax.axis_index("clip")
    f = lax.axis_index("frame")
    other = 1 - c
    block = w_hbm.shape[0]
    tok = q_hbm.shape[1]
    sub = tok // N_FRAME
    n_block = w0.shape[0]
    n_z = AX["z"][0]
    last = n_z - 1
    scale = 1.0 / math.sqrt(HDIM)
    x = lax.rem(f, 2)
    pair = lax.div(f, 2)
    y = lax.rem(pair, 2)
    z = lax.div(pair, 2)
    beside = f + 1 - 2 * x
    across = move(f, "y", 1)
    slot = x * 2 + c

    def remote(src, dst, ss, rs, peer):
        pltpu.make_async_remote_copy(
            src_ref=src, dst_ref=dst, send_sem=ss, recv_sem=rs,
            device_id=peer, device_id_type=pl.DeviceIdType.MESH,
        ).start()

    def local(src, dst, sem):
        pltpu.make_async_copy(src, dst, sem).start()

    def wait(view, sem):
        pltpu.make_async_copy(view, view, sem).wait()

    def on_core(fn):
        for core in range(2):
            pl.when(c == core)(functools.partial(fn, core))

    barrier = pltpu.get_barrier_semaphore()

    def greet(peer):
        pl.semaphore_signal(barrier, inc=1, device_id=peer, device_id_type=pl.DeviceIdType.MESH)

    @pl.loop(1, N_FRAME)
    def _(d):
        greet((c, lax.rem(f + d, N_FRAME)))

    greet((other, f))
    greet((other, beside))

    turned = ((q_hbm, tq), (k_hbm, tk), (g_hbm, tg), (v_hbm, tv))
    pairs = ((sq, qb), (sk, kb), (sg, gb), (sv, vb))
    for i, (src, flat) in enumerate(turned):
        local(src, flat, t_sem.at[i])
    local(h_hbm, hb, loc.at[0])
    w_part = (w0, w1)
    for i in range(2):
        local(w_hbm.at[:, slice(*W_COLS[i])], w_part[i].at[pair], loc.at[1 + i])
    pl.semaphore_wait(barrier, N_FRAME + 1)

    def w_at(core, zb, yb):
        return w_part[core].at[zb * 2 + yb]

    def forward(core, zb, yb):
        remote(w_at(core, zb, yb), w_at(core, zb, yb), wc_send, wc_recv, (other, f))

    def pass_y(core, zb, src=None):
        dst = w_at(core, zb, y)
        remote(dst if src is None else src, dst, wy_send, wy_recv.at[zb], (c, across))

    def climb(core, zb, way, src=None):
        dst = w_at(core, zb, y)

        @pl.when((z < last) if way == 1 else (z > 0))
        def _():
            remote(dst if src is None else src, dst, wz_send, wz_recv.at[zb], (c, f + way * AX["z"][1]))

    def own(core):
        return w_hbm.at[:, slice(*W_COLS[core])]

    def w_start_y(core):
        pass_y(core, z, own(core))

    def w_start_z(core):
        for way in (1, -1):
            climb(core, z, way, own(core))

    def w_hop(h, core):
        for way in (1, -1):
            from_z = z - way * h

            @pl.when((from_z >= 0) & (from_z <= last))
            def _():
                wait(w_part[core].at[0], wz_recv.at[from_z])
                climb(core, from_z, way)
                pass_y(core, from_z)
                forward(core, from_z, y)

    def w_y0(core):
        wait(w_part[core].at[0], wy_recv.at[z])
        forward(core, z, 1 - y)

    def w_ys(core):
        for k in range(1, n_z):
            zb = lax.rem(z + k, n_z)
            wait(w_part[core].at[0], wy_recv.at[zb])
            forward(core, zb, 1 - y)

    def w_drain(core):
        wait(w_part[core].at[pl.ds(0, n_z)], wy_send)
        edge = (z == 0) | (z == last)
        for ends, count in ((True, 1), (False, 5)):

            @pl.when(edge if ends else jnp.logical_not(edge))
            def _():
                wait(w_part[core].at[pl.ds(0, count)], wz_send)

        wait(w_part[core].at[pl.ds(0, n_block - 1)], wc_send)

    on_core(w_start_y)
    for i, (src, dst) in enumerate(pairs):
        pltpu.make_async_copy(turned[i][0], turned[i][1], t_sem.at[i]).wait()
        src[...] = turned[i][1][...].T.reshape(src.shape)
        local(src.at[f], dst.at[f], a_recv.at[i])

        @pl.loop(1, N_FRAME)
        def _(d):
            to = lax.rem(f + d, N_FRAME)
            remote(src.at[to], dst.at[f], a_send.at[i], a_recv.at[i], (c, to))

    on_core(w_start_z)

    acc_q[...] = jnp.zeros_like(acc_q)
    acc_k[...] = jnp.zeros_like(acc_k)
    acc_v[...] = jnp.zeros_like(acc_v)
    row_id = lax.broadcasted_iota(jnp.int32, (tok, tok), 0)
    col_id = lax.broadcasted_iota(jnp.int32, (tok, tok), 1)
    same = lax.rem(row_id, sub) == lax.rem(col_id, sub)

    width_all = q_hbm.shape[0]
    heads = width_all // HDIM
    nt = (((1,), (1,)), ((), ()))
    tn = (((0,), (0,)), ((), ()))
    nn = (((1,), (0,)), ((), ()))
    dot = functools.partial(lax.dot_general, preferred_element_type=jnp.float32)

    def window(n):
        low = n * HDIM // 128 * 128
        high = min(-(-(n + 1) * HDIM // 128) * 128, width_all)
        lane = lax.broadcasted_iota(jnp.int32, (tok, high - low), 1) + low
        keep = jnp.where((lane >= n * HDIM) & (lane < (n + 1) * HDIM), 1.0, 0.0)
        return slice(low, high), keep.astype(jnp.bfloat16)

    def rows(ref, win):
        return ref[:, :, win].reshape(tok, win.stop - win.start)

    probs = []

    def hidden():
        pltpu.make_async_copy(h_hbm, hb, loc.at[0]).wait()
        for k in range(2):
            half = jnp.concatenate(
                [hb[:, (2 * i + k) * block : (2 * i + k + 1) * block] for i in range(n_block)], axis=1
            )
            hs[k] = half
        hall[slot] = hs[x]
        remote(hs.at[1 - x], hall.at[slot], h_send.at[0], h_recv.at[0], (c, beside))
        remote(hs.at[x], hall.at[slot], h_send.at[1], h_recv.at[1], (other, f))

    def spread():
        theirs = hall.at[(1 - x) * 2 + c]
        wait(theirs, h_recv.at[0])
        remote(theirs, theirs, h_send.at[2], h_recv.at[2], (other, f))

    def attend_v():
        for i, ref in enumerate((qb, kb, gb)):
            wait(ref, a_recv.at[i])
        for n in range(heads):
            win, keep = window(n)
            s = dot(rows(qb, win) * keep, rows(kb, win), nt) * scale
            s = jnp.where(same, s, -1e30)
            e = jnp.exp(s - jnp.max(s, axis=1, keepdims=True))
            p = e / jnp.sum(e, axis=1, keepdims=True)
            probs.append(p)
            acc_v[:, win] += dot(p.astype(jnp.bfloat16), rows(gb, win) * keep, tn)
        out_v[...] = acc_v[...].astype(jnp.bfloat16).reshape(out_v.shape)
        local(out_v.at[f], gall.at[slot, f], b_recv)

        @pl.loop(1, N_FRAME)
        def _(d):
            to = lax.rem(f + d, N_FRAME)
            remote(out_v.at[to], gall.at[lax.rem(to, 2) * 2 + c, f], b_send, b_recv, (c, to))

    def attend_qk():
        wait(vb, a_recv.at[3])
        for n in range(heads):
            win, keep = window(n)
            p = probs[n]
            dp = dot(rows(gb, win) * keep, rows(vb, win), nt)
            ds = (p * (dp - jnp.sum(p * dp, axis=1, keepdims=True))).astype(jnp.bfloat16)
            acc_q[:, win] += dot(ds, rows(kb, win) * keep, nn)
            acc_k[:, win] += dot(ds, rows(qb, win) * keep, tn)
        cat[x] = jnp.concatenate(
            [
                (acc_q[...] * scale).astype(jnp.bfloat16),
                (acc_k[...] * scale).astype(jnp.bfloat16),
                acc_v[...].astype(jnp.bfloat16),
            ],
            axis=1,
        )

    def swap():
        remote(cat.at[x], cat.at[x], x_sem.at[0], x_sem.at[1], (c, beside))

    def share(core):
        wait(gall.at[0], b_recv)
        for to in range(2):
            src = gall.at[slot, :, :, slice(*COLS[to])]
            remote(src, src, g_send.at[to], g_recv.at[0 if to == core else 1], (to, beside))
            if to != core:
                remote(src, src, g_send.at[2], g_recv.at[2], (to, f))

    def weight(core):
        cols = slice(*COLS[core])
        wait(hall.at[0], h_recv.at[1])
        wait(hall.at[0], h_recv.at[2])
        for i in range(3):
            wait(gall.at[0, :, :, cols], g_recv.at[i])
        n = cols.stop - cols.start
        total = dot(hall[...].reshape(4 * tok, hall.shape[2]), gall[:, :, :, cols].reshape(4 * tok, n), tn)
        dws[:, :, cols] = total.reshape(n_block, block, n)
        for zb in range(n_z):
            y_s[zb, :, cols] = dws[zb * 2 + 1 - y, :, cols].astype(jnp.bfloat16)
        remote(y_s.at[:, :, cols], y_r.at[:, :, cols], ry_sem.at[0], ry_sem.at[1], (c, across))

    def sum_y(core):
        cols = slice(*COLS[core])
        wait(y_r.at[:, :, cols], ry_sem.at[1])
        for k in range(1, n_z):
            zb = lax.rem(z + k, n_z)
            total = dws[zb * 2 + y, :, cols] + y_r[zb, :, cols].astype(jnp.float32)
            z_s[zb, :, cols] = total.astype(jnp.bfloat16)
            remote(z_s.at[zb, :, cols], z_r.at[z, :, cols], rz_send, rz_recv, (c, move(f, "z", k)))
        dws[pair, :, cols] += y_r[z, :, cols].astype(jnp.float32)

    def sum_z(core):
        cols = slice(*COLS[core])
        wait(z_r.at[pl.ds(0, n_z - 1), :, cols], rz_recv)
        total = dws[pair, :, cols]
        for k in range(1, n_z):
            total += z_r[lax.rem(z + k, n_z), :, cols].astype(jnp.float32)
        total *= 0.5
        fin_s[:, cols] = total
        remote(fin_s.at[:, cols], fin_r.at[:, cols], f_sem.at[0], f_sem.at[1], (other, f))
        gw_ref[:, cols] = total

    def finish(core):
        mine, rest = slice(*COLS[core]), slice(*COLS[1 - core])
        wait(fin_r.at[:, rest], f_sem.at[1])
        gw_ref[:, rest] = fin_r[:, rest]
        wait(fin_s.at[:, mine], f_sem.at[0])
        wait(y_s.at[:, :, mine], ry_sem.at[0])
        wait(z_s.at[pl.ds(0, n_z - 1), :, mine], rz_send)
        for to in range(2):
            wait(gall.at[0, :, :, slice(*COLS[to])], g_send.at[to])
            if to != core:
                wait(gall.at[0, :, :, slice(*COLS[to])], g_send.at[2])
        w_drain(core)

    def w_last(core):
        wait(w_part[1 - core].at[pl.ds(0, n_block - 1)], wc_recv)

    def project():
        wait(cat.at[0], x_sem.at[1])
        for i in range(2):
            pltpu.make_async_copy(w_hbm.at[:, slice(*W_COLS[i])], w_part[i].at[pair], loc.at[1 + i]).wait()
        on_core(w_last)
        grads = cat[...].reshape(2 * tok, cat.shape[2])
        parts = [w[...].reshape(n_block * block, w.shape[2]) for w in w_part]
        for low, high in CHUNKS:
            res = sum(dot(grads[:, slice(*W_COLS[i])], parts[i][low:high], nt) for i in range(2))
            ob[:, :, :, low:high] = res.astype(jnp.bfloat16).reshape(2, N_FRAME, sub, high - low)
            dst = land.at[x, pl.ds(pair * 2, 2), :, low:high]
            local(ob.at[:, f, :, low:high], dst, o_recv)

            @pl.loop(1, N_FRAME)
            def _(d):
                to = lax.rem(f + d, N_FRAME)
                remote(ob.at[:, to, :, low:high], dst, o_send, o_recv, (c, to))

    def collect():
        wait(land, o_recv)
        halves = [land[k].reshape(tok, land.shape[3]) for k in range(2)]
        gh_ref[...] = jnp.concatenate(
            [halves[k][:, i * block : (i + 1) * block] for i in range(n_block) for k in range(2)], axis=1
        )

    steps = {
        "hidden": hidden, "spread": spread, "attend_v": attend_v, "attend_qk": attend_qk, "swap": swap,
        "project": project, "collect": collect,
    }
    for name, fn in (
        ("y0", w_y0), ("ys", w_ys), ("share", share), ("weight", weight), ("sum_y", sum_y),
        ("sum_z", sum_z), ("finish", finish),
    ):
        steps[name] = functools.partial(on_core, fn)
    for i in range(1, n_z):
        steps["hop" + str(i)] = functools.partial(on_core, functools.partial(w_hop, i))
    for name in ORDER:
        steps[name]()

    for i, (src, _) in enumerate(pairs):
        wait(src.at[pl.ds(0, N_FRAME - 1)], a_send.at[i])
    wait(out_v.at[pl.ds(0, N_FRAME - 1)], b_send)
    wait(cat.at[0], x_sem.at[0])
    wait(ob.at[:, pl.ds(0, N_FRAME - 1)], o_send)
    for i in range(3):
        wait(hs.at[0], h_send.at[i])


def per_device_fused(hidden, queries, keys, values, grad_attn, w_qkv):
    tok, width = hidden.shape[2], hidden.shape[3]
    inner = queries.shape[3]
    block, cat_w = w_qkv.shape
    flat = [
        jnp.swapaxes(a.reshape(tok, inner), 0, 1) for a in (queries, keys, values, grad_attn)
    ]
    bf, f32 = jnp.bfloat16, jnp.float32
    dma = pltpu.SemaphoreType.DMA
    sub, n_block, half = tok // N_FRAME, N_FRAME // 2, width // 2
    n_z = AX["z"][0]
    vmem = pltpu.VMEM
    scratch = (
        [vmem((inner, tok), bf)] * 4
        + [vmem((N_FRAME, sub, inner), bf)] * 8
        + [vmem((tok, width), bf), vmem((2, tok, half), bf), vmem((4, tok, half), bf)]
        + [vmem((n_block, block, high - low), bf) for low, high in W_COLS]
        + [vmem((tok, inner), f32)] * 3
        + [vmem((N_FRAME, sub, inner), bf), vmem((4, N_FRAME, sub, inner), bf), vmem((2, tok, cat_w), bf)]
        + [vmem((2, N_FRAME, sub, half), bf)] * 2
        + [vmem((n_block, block, inner), f32)]
        + [vmem((n_z, block, inner), bf)] * 4
        + [vmem((block, inner), f32)] * 2
        + [dma((3,)), dma((4,)), dma((4,)), dma((4,)), dma, dma, dma, dma((n_z,)), dma, dma((n_z,)), dma, dma]
        + [dma((3,)), dma((3,)), dma((2,)), dma((3,)), dma((3,)), dma, dma, dma((2,)), dma, dma, dma((2,))]
    )
    grad_hidden, grad_w = pl.pallas_call(
        kernel,
        out_shape=(
            jax.ShapeDtypeStruct((tok, width), bf),
            jax.ShapeDtypeStruct((block, inner), f32),
        ),
        in_specs=[pl.BlockSpec(memory_space=pl.ANY)] * 6,
        out_specs=(pl.BlockSpec(memory_space=pltpu.VMEM),) * 2,
        scratch_shapes=scratch,
        compiler_params=pltpu.CompilerParams(
            collective_id=0, has_side_effects=True, vmem_limit_bytes=60 * 1024 * 1024
        ),
    )(*flat, hidden.reshape(tok, width), w_qkv)
    return grad_hidden.reshape(hidden.shape), grad_w


def solution(mesh):
    in_specs = (
        P("clip", "frame", None, None),
        P("clip", "frame", None, None),
        P("clip", "frame", None, None),
        P("clip", "frame", None, None),
        P("clip", "frame", None, None),
        P("frame", None),
    )
    out_specs = (P("clip", "frame", None, None), P("frame", None))
    fused = mesh.shape["clip"] == 2 and mesh.shape["frame"] == N_FRAME
    return jax.shard_map(
        per_device_fused if fused else per_device, mesh=mesh, in_specs=in_specs, out_specs=out_specs, check_vma=False
    )
```

```python
import functools
import math

import jax
import jax.numpy as jnp
from jax import lax
from jax.experimental import pallas as pl
from jax.experimental.pallas import tpu as pltpu
from jax.sharding import PartitionSpec as P

HDIM = 104


def attend_back(queries, keys, values, grad_out):
    score_scale = 1.0 / math.sqrt(HDIM)
    scores = (
        jnp.einsum("fpnd,gpnd->pnfg", queries, keys, preferred_element_type=jnp.float32)
        * score_scale
    )
    attn_probs = jax.nn.softmax(scores, axis=-1)
    probs_bf = attn_probs.astype(jnp.bfloat16)
    grad_v = jnp.einsum(
        "pnfg,fpnd->gpnd", probs_bf, grad_out, preferred_element_type=jnp.float32
    ).astype(jnp.bfloat16)
    grad_probs = jnp.einsum("fpnd,gpnd->pnfg", grad_out, values, preferred_element_type=jnp.float32)
    grad_scores = attn_probs * (
        grad_probs - jnp.sum(attn_probs * grad_probs, axis=-1, keepdims=True)
    )
    scores_bf = grad_scores.astype(jnp.bfloat16)
    grad_q = (
        jnp.einsum("pnfg,gpnd->fpnd", scores_bf, keys, preferred_element_type=jnp.float32)
        * score_scale
    ).astype(jnp.bfloat16)
    grad_k = (
        jnp.einsum("pnfg,fpnd->gpnd", scores_bf, queries, preferred_element_type=jnp.float32)
        * score_scale
    ).astype(jnp.bfloat16)
    return (grad_q, grad_k, grad_v)


def per_device(hidden, queries, keys, values, grad_attn, w_qkv):
    frames_local = hidden.shape[1]
    patches = hidden.shape[2]
    model_width = hidden.shape[3]
    inner_width = queries.shape[3]
    head_count = inner_width // HDIM
    row_count = frames_local * patches
    head_shape = (frames_local, patches, head_count, HDIM)
    q_local = queries.reshape(head_shape)
    k_local = keys.reshape(head_shape)
    v_local = values.reshape(head_shape)
    g_local = grad_attn.reshape(head_shape)
    q_patch, k_patch, v_patch, g_patch = (
        lax.all_to_all(q_local, "frame", split_axis=1, concat_axis=0, tiled=True),
        lax.all_to_all(k_local, "frame", split_axis=1, concat_axis=0, tiled=True),
        lax.all_to_all(v_local, "frame", split_axis=1, concat_axis=0, tiled=True),
        lax.all_to_all(g_local, "frame", split_axis=1, concat_axis=0, tiled=True),
    )
    grad_q, grad_k, grad_v = attend_back(q_patch, k_patch, v_patch, g_patch)
    grad_q, grad_k, grad_v = (
        lax.all_to_all(grad_q, "frame", split_axis=0, concat_axis=1, tiled=True),
        lax.all_to_all(grad_k, "frame", split_axis=0, concat_axis=1, tiled=True),
        lax.all_to_all(grad_v, "frame", split_axis=0, concat_axis=1, tiled=True),
    )
    value_rows = grad_v.reshape(row_count, inner_width)
    grad_cat = jnp.concatenate(
        [
            grad_q.reshape(row_count, inner_width),
            grad_k.reshape(row_count, inner_width),
            value_rows,
        ],
        axis=1,
    )
    grad_hid = lax.dot_general(
        grad_cat,
        lax.all_gather(w_qkv, "frame", axis=0, tiled=True),
        (((1,), (1,)), ((), ())),
        preferred_element_type=jnp.float32,
    )
    grad_hidden = grad_hid.astype(jnp.bfloat16).reshape(hidden.shape)
    hidden_rows = hidden.reshape(row_count, model_width)
    clip_count = lax.axis_size("clip")
    partial_grad = lax.psum_scatter(
        lax.dot_general(
            hidden_rows, value_rows, (((0,), (0,)), ((), ())), preferred_element_type=jnp.float32
        ),
        "frame",
        scatter_dimension=0,
        tiled=True,
    )
    grad_total = lax.psum(partial_grad, "clip")
    return (grad_hidden, grad_total / clip_count)


AX = {"z": (4, 4), "y": (2, 2), "x": (2, 1)}
N_FRAME = 16
ORDER = (
    "own_y", "own_z", "turn", "plane", "a00", "enter1", "a01", "enter2", "a02", "enter3", "a03",
    "a10", "a11", "a12", "a13", "hop1", "hidden", "spread", "y0", "attend0", "attend1",
    "hop2", "share0", "share1", "hop3", "y1", "y2", "y3", "weight", "project0", "project1", "project2",
    "project3", "sum_y", "sum_z", "finish", "collect",
)
NEAR = (1, 2, 0, 3)
COLS = ((0, 384), (384, 832))
PARTS = ((0, 512), (512, 832))
W_COLS = ((0, 1280), (1280, 2496))


def move(f, axis, k):
    size, stride = AX[axis]
    digit = lax.rem(lax.div(f, stride), size)
    return f + (lax.rem(digit + k, size) - digit) * stride


def kernel(
    q_hbm, k_hbm, v_hbm, g_hbm, h_hbm, w_hbm,
    gh_ref, gw_ref,
    tq, tk, tv, tg, leaving, arrived,
    hb, hs, hall, w0, w1, acc_q, acc_k, acc_v, out_v, gall, cat, joined, ob, land,
    dws, y_s, y_r, z_s, z_r, fin_s, fin_r,
    loc, t_sem, a_send, a_recv, b_send, b_recv, wy_send, wy_recv, wz_send, wz_recv, wc_send, wc_recv,
    h_send, h_recv, x_sem, g_send, g_recv, o_send, o_recv, ry_sem, rz_send, rz_recv, f_sem, plane_sem, in_sem,
):
    c = lax.axis_index("clip")
    f = lax.axis_index("frame")
    other = 1 - c
    block = w_hbm.shape[0]
    tok = q_hbm.shape[1]
    sub = tok // N_FRAME
    n_block = w0.shape[0]
    n_z = AX["z"][0]
    last = n_z - 1
    scale = 1.0 / math.sqrt(HDIM)
    x = lax.rem(f, 2)
    pair = lax.div(f, 2)
    y = lax.rem(pair, 2)
    z = lax.div(pair, 2)
    beside = f + 1 - 2 * x
    across = move(f, "y", 1)
    slot = x * 2 + c

    def remote(src, dst, ss, rs, peer):
        pltpu.make_async_remote_copy(
            src_ref=src, dst_ref=dst, send_sem=ss, recv_sem=rs,
            device_id=peer, device_id_type=pl.DeviceIdType.MESH,
        ).start()

    def local(src, dst, sem):
        pltpu.make_async_copy(src, dst, sem).start()

    def wait(view, sem):
        pltpu.make_async_copy(view, view, sem).wait()

    def on_core(fn):
        for core in range(2):
            pl.when(c == core)(functools.partial(fn, core))

    barrier = pltpu.get_barrier_semaphore()

    def greet(peer):
        pl.semaphore_signal(barrier, inc=1, device_id=peer, device_id_type=pl.DeviceIdType.MESH)

    for peer in ((c, beside), (c, across), (other, f), (other, beside)):
        greet(peer)
    for way in (1, -1):

        @pl.when((z < last) if way == 1 else (z > 0))
        def _():
            greet((c, f + way * AX["z"][1]))

    turned = ((q_hbm, tq), (k_hbm, tk), (g_hbm, tg), (v_hbm, tv))
    pairs = [(leaving.at[i], arrived.at[i]) for i in range(4)]
    qb, kb, gb, vb = (arrived.at[i] for i in range(4))
    for i, (src, flat) in enumerate(turned):
        local(src, flat, t_sem.at[i])
    local(h_hbm, hb, loc.at[0])
    w_part = (w0, w1)
    for i in range(2):
        local(w_hbm.at[:, slice(*W_COLS[i])], w_part[i].at[pair], loc.at[1 + i])
    pl.semaphore_wait(barrier, 6 - jnp.where((z == 0) | (z == last), 1, 0))

    def tell(sem, peer):
        pl.semaphore_signal(sem, inc=1, device_id=peer, device_id_type=pl.DeviceIdType.MESH)

    def pass_in(from_z, way):
        @pl.when((z < last) if way == 1 else (z > 0))
        def _():
            tell(in_sem.at[from_z], (c, f + way * AX["z"][1]))

    def plane():
        tell(plane_sem, (c, across))
        pl.semaphore_wait(plane_sem, 1)
        for way in (1, -1):
            pass_in(z, way)

    def enter(h):
        for way in (1, -1):
            from_z = z - way * h

            @pl.when((from_z >= 0) & (from_z <= last))
            def _():
                pl.semaphore_wait(in_sem.at[from_z], 1)
                pass_in(from_z, way)

    def w_at(core, zb, yb):
        return w_part[core].at[zb * 2 + yb]

    def forward(core, zb, yb):
        remote(w_at(core, zb, yb), w_at(core, zb, yb), wc_send, wc_recv.at[zb], (other, f))

    def pass_y(core, zb, src=None):
        dst = w_at(core, zb, y)
        remote(dst if src is None else src, dst, wy_send, wy_recv.at[zb], (c, across))

    def climb(core, zb, way, src=None):
        dst = w_at(core, zb, y)

        @pl.when((z < last) if way == 1 else (z > 0))
        def _():
            remote(dst if src is None else src, dst, wz_send, wz_recv.at[zb], (c, f + way * AX["z"][1]))

    def own(core):
        return w_hbm.at[:, slice(*W_COLS[core])]

    def w_start_y(core):
        pass_y(core, z, own(core))

    def w_start_z(core):
        for way in (1, -1):
            climb(core, z, way, own(core))

    def w_hop(h, core):
        for way in (1, -1):
            from_z = z - way * h

            @pl.when((from_z >= 0) & (from_z <= last))
            def _():
                wait(w_part[core].at[0], wz_recv.at[from_z])
                climb(core, from_z, way)
                pass_y(core, from_z)
                forward(core, from_z, y)

    def w_y0(core):
        wait(w_part[core].at[0], wy_recv.at[z])
        forward(core, z, 1 - y)

    def by_distance(j):
        at_end = (z == 0) | (z == last)
        up = jnp.where(at_end, j, NEAR[j])
        return jnp.where(z * 2 < n_z, up, last - up)

    def w_ys(j, core):
        zb = by_distance(j)
        wait(w_part[core].at[0], wy_recv.at[zb])
        forward(core, zb, 1 - y)

    def w_drain(core):
        wait(w_part[core].at[pl.ds(0, n_z)], wy_send)
        edge = (z == 0) | (z == last)
        for ends, count in ((True, 1), (False, 5)):

            @pl.when(edge if ends else jnp.logical_not(edge))
            def _():
                wait(w_part[core].at[pl.ds(0, count)], wz_send)

        wait(w_part[core].at[pl.ds(0, n_block - 1)], wc_send)

    def turn():
        for i, (src, _) in enumerate(pairs):
            pltpu.make_async_copy(turned[i][0], turned[i][1], t_sem.at[i]).wait()
            src[...] = turned[i][1][...].T.reshape(src.shape)

    def exchange(part, h):
        cols = slice(*PARTS[part])

        def to_frame(to):
            for src, dst in pairs:
                remote(src.at[to, :, cols], dst.at[f, :, cols], a_send.at[part], a_recv.at[part], (c, to))

        if h == 0:
            for src, dst in pairs:
                local(src.at[f, :, cols], dst.at[f, :, cols], a_recv.at[part])
            for to in (beside, across, move(across, "x", 1)):
                to_frame(to)
            return
        for way in (1, -1):
            to_z = z - way * h

            @pl.when((to_z >= 0) & (to_z <= last))
            def _():
                @pl.loop(0, AX["z"][1])
                def _(k):
                    to_frame(to_z * AX["z"][1] + k)

    acc_q[...] = jnp.zeros_like(acc_q)
    acc_k[...] = jnp.zeros_like(acc_k)
    acc_v[...] = jnp.zeros_like(acc_v)
    row_id = lax.broadcasted_iota(jnp.int32, (tok, tok), 0)
    col_id = lax.broadcasted_iota(jnp.int32, (tok, tok), 1)
    same = lax.rem(row_id, sub) == lax.rem(col_id, sub)

    width_all = q_hbm.shape[0]
    heads = width_all // HDIM
    nt = (((1,), (1,)), ((), ()))
    tn = (((0,), (0,)), ((), ()))
    nn = (((1,), (0,)), ((), ()))
    dot = functools.partial(lax.dot_general, preferred_element_type=jnp.float32)

    def window(n):
        low = n * HDIM // 128 * 128
        high = min(-(-(n + 1) * HDIM // 128) * 128, width_all)
        lane = lax.broadcasted_iota(jnp.int32, (tok, high - low), 1) + low
        keep = jnp.where((lane >= n * HDIM) & (lane < (n + 1) * HDIM), 1.0, 0.0)
        return slice(low, high), keep.astype(jnp.bfloat16)

    def rows(ref, win):
        return ref[:, :, win].reshape(tok, win.stop - win.start)

    def hidden():
        pltpu.make_async_copy(h_hbm, hb, loc.at[0]).wait()
        for k in range(2):
            half = jnp.concatenate(
                [hb[:, (2 * i + k) * block : (2 * i + k + 1) * block] for i in range(n_block)], axis=1
            )
            hs[k] = half
        hall[slot] = hs[x]
        remote(hs.at[1 - x], hall.at[slot], h_send.at[0], h_recv.at[0], (c, beside))
        remote(hs.at[x], hall.at[slot], h_send.at[1], h_recv.at[1], (other, f))

    def spread():
        theirs = hall.at[(1 - x) * 2 + c]
        wait(theirs, h_recv.at[0])
        remote(theirs, theirs, h_send.at[2], h_recv.at[2], (other, f))

    def attend(part):
        wait(arrived.at[:, :, :, slice(*PARTS[part])], a_recv.at[part])
        half = heads // 2
        for n in range(part * half, (part + 1) * half):
            win, keep = window(n)
            g = rows(gb, win) * keep
            s = dot(rows(qb, win) * keep, rows(kb, win), nt) * scale
            s = jnp.where(same, s, -1e30)
            e = jnp.exp(s - jnp.max(s, axis=1, keepdims=True))
            p = e / jnp.sum(e, axis=1, keepdims=True)
            acc_v[:, win] += dot(p.astype(jnp.bfloat16), g, tn)
            dp = dot(g, rows(vb, win), nt)
            ds = (p * (dp - jnp.sum(p * dp, axis=1, keepdims=True))).astype(jnp.bfloat16)
            acc_q[:, win] += dot(ds, rows(kb, win) * keep, nn)
            acc_k[:, win] += dot(ds, rows(qb, win) * keep, tn)
        cols = slice(*COLS[part])
        grad_v = acc_v[:, cols].astype(jnp.bfloat16)
        out_v[:, :, cols] = grad_v.reshape(N_FRAME, sub, cols.stop - cols.start)
        local(out_v.at[f, :, cols], gall.at[slot, f, :, cols], b_recv.at[part])

        @pl.loop(1, N_FRAME)
        def _(d):
            to = lax.rem(f + d, N_FRAME)
            dst = gall.at[lax.rem(to, 2) * 2 + c, f, :, cols]
            remote(out_v.at[to, :, cols], dst, b_send.at[part], b_recv.at[part], (c, to))

        cat[x, 0, :, cols] = (acc_q[:, cols] * scale).astype(jnp.bfloat16)
        cat[x, 1, :, cols] = (acc_k[:, cols] * scale).astype(jnp.bfloat16)
        cat[x, 2, :, cols] = grad_v
        mine = cat.at[x, :, :, cols]
        remote(mine, mine, x_sem.at[0, part], x_sem.at[1, part], (c, beside))

    def share(to, core):
        wait(gall.at[0, :, :, slice(*COLS[to])], b_recv.at[to])
        src = gall.at[slot, :, :, slice(*COLS[to])]
        remote(src, src, g_send.at[to], g_recv.at[0 if to == core else 1], (to, beside))
        if to != core:
            remote(src, src, g_send.at[2], g_recv.at[2], (to, f))

    def weight(core):
        cols = slice(*COLS[core])
        wait(hall.at[0], h_recv.at[1])
        wait(hall.at[0], h_recv.at[2])
        for i in range(3):
            wait(gall.at[0, :, :, cols], g_recv.at[i])
        n = cols.stop - cols.start
        total = dot(hall[...].reshape(4 * tok, hall.shape[2]), gall[:, :, :, cols].reshape(4 * tok, n), tn)
        dws[:, :, cols] = total.reshape(n_block, block, n)
        for zb in range(n_z):
            y_s[zb, :, cols] = dws[zb * 2 + 1 - y, :, cols].astype(jnp.bfloat16)
        remote(y_s.at[:, :, cols], y_r.at[:, :, cols], ry_sem.at[0], ry_sem.at[1], (c, across))

    def sum_y(core):
        cols = slice(*COLS[core])
        wait(y_r.at[:, :, cols], ry_sem.at[1])
        for k in range(1, n_z):
            zb = lax.rem(z + k, n_z)
            total = dws[zb * 2 + y, :, cols] + y_r[zb, :, cols].astype(jnp.float32)
            z_s[zb, :, cols] = total.astype(jnp.bfloat16)
            remote(z_s.at[zb, :, cols], z_r.at[z, :, cols], rz_send, rz_recv, (c, move(f, "z", k)))
        dws[pair, :, cols] += y_r[z, :, cols].astype(jnp.float32)

    def sum_z(core):
        cols = slice(*COLS[core])
        wait(z_r.at[pl.ds(0, n_z - 1), :, cols], rz_recv)
        total = dws[pair, :, cols]
        for k in range(1, n_z):
            total += z_r[lax.rem(z + k, n_z), :, cols].astype(jnp.float32)
        total *= 0.5
        fin_s[:, cols] = total
        remote(fin_s.at[:, cols], fin_r.at[:, cols], f_sem.at[0], f_sem.at[1], (other, f))
        gw_ref[:, cols] = total

    def finish(core):
        mine, rest = slice(*COLS[core]), slice(*COLS[1 - core])
        wait(fin_r.at[:, rest], f_sem.at[1])
        gw_ref[:, rest] = fin_r[:, rest]
        wait(fin_s.at[:, mine], f_sem.at[0])
        wait(y_s.at[:, :, mine], ry_sem.at[0])
        wait(z_s.at[pl.ds(0, n_z - 1), :, mine], rz_send)
        for to in range(2):
            wait(gall.at[0, :, :, slice(*COLS[to])], g_send.at[to])
            if to != core:
                wait(gall.at[0, :, :, slice(*COLS[to])], g_send.at[2])
        w_drain(core)

    def project(j):
        zb = by_distance(j)
        if j == 0:
            for i in range(2):
                wait(cat.at[0, :, :, slice(*COLS[i])], x_sem.at[1, i])
                pltpu.make_async_copy(w_hbm.at[:, slice(*W_COLS[i])], w_part[i].at[pair], loc.at[1 + i]).wait()
        on_core(lambda core: wait(w_part[1 - core].at[pl.ds(0, 2 if j else 1)], wc_recv.at[zb]))
        if j == 0:
            for k in range(2):
                joined[k] = jnp.concatenate([cat[k, i] for i in range(3)], axis=1)
        grads = joined[...].reshape(2 * tok, joined.shape[2])
        parts = [w[pl.ds(zb * 2, 2)].reshape(2 * block, w.shape[2]) for w in w_part]
        res = sum(dot(grads[:, slice(*W_COLS[i])], parts[i], nt) for i in range(2))
        ob[zb] = res.astype(jnp.bfloat16).reshape(2, N_FRAME, sub, 2 * block)
        dst = land.at[x, zb, pl.ds(pair * 2, 2)]
        local(ob.at[zb, :, f], dst, o_recv)

        @pl.loop(1, N_FRAME)
        def _(d):
            to = lax.rem(f + d, N_FRAME)
            remote(ob.at[zb, :, to], dst, o_send, o_recv, (c, to))

    def collect():
        wait(land, o_recv)
        pieces = [
            land[k, zb][:, :, yb * block : (yb + 1) * block].reshape(tok, block)
            for zb in range(n_z) for yb in range(2) for k in range(2)
        ]
        gh_ref[...] = jnp.concatenate(pieces, axis=1)

    steps = {
        "hidden": hidden, "spread": spread, "turn": turn, "plane": plane,
        "collect": collect,
    }
    for i in range(2):
        for h in range(n_z):
            steps["a" + str(i) + str(h)] = functools.partial(exchange, i, h)
        steps["attend" + str(i)] = functools.partial(attend, i)
        steps["share" + str(i)] = functools.partial(on_core, functools.partial(share, i))
    for name, fn in (
        ("own_y", w_start_y), ("own_z", w_start_z), ("y0", w_y0), ("ys", w_ys), ("weight", weight), ("sum_y", sum_y),
        ("sum_z", sum_z), ("finish", finish),
    ):
        steps[name] = functools.partial(on_core, fn)
    for i in range(1, n_z):
        steps["hop" + str(i)] = functools.partial(on_core, functools.partial(w_hop, i))
        steps["enter" + str(i)] = functools.partial(enter, i)
        steps["y" + str(i)] = functools.partial(on_core, functools.partial(w_ys, i))
    for j in range(n_z):
        steps["project" + str(j)] = functools.partial(project, j)
    for name in ORDER:
        steps[name]()

    for i in range(2):
        wait(leaving.at[:, pl.ds(0, N_FRAME - 1), :, slice(*PARTS[i])], a_send.at[i])
        wait(out_v.at[pl.ds(0, N_FRAME - 1), :, slice(*COLS[i])], b_send.at[i])
        wait(cat.at[0, :, :, slice(*COLS[i])], x_sem.at[0, i])
    wait(ob.at[:, :, pl.ds(0, N_FRAME - 1)], o_send)
    for i in range(3):
        wait(hs.at[0], h_send.at[i])


def per_device_fused(hidden, queries, keys, values, grad_attn, w_qkv):
    tok, width = hidden.shape[2], hidden.shape[3]
    inner = queries.shape[3]
    block, cat_w = w_qkv.shape
    flat = [
        jnp.swapaxes(a.reshape(tok, inner), 0, 1) for a in (queries, keys, values, grad_attn)
    ]
    bf, f32 = jnp.bfloat16, jnp.float32
    dma = pltpu.SemaphoreType.DMA
    sub, n_block, half = tok // N_FRAME, N_FRAME // 2, width // 2
    n_z = AX["z"][0]
    vmem = pltpu.VMEM
    scratch = (
        [vmem((inner, tok), bf)] * 4
        + [vmem((4, N_FRAME, sub, inner), bf)] * 2
        + [vmem((tok, width), bf), vmem((2, tok, half), bf), vmem((4, tok, half), bf)]
        + [vmem((n_block, block, high - low), bf) for low, high in W_COLS]
        + [vmem((tok, inner), f32)] * 3
        + [vmem((N_FRAME, sub, inner), bf), vmem((4, N_FRAME, sub, inner), bf)]
        + [vmem((2, 3, tok, inner), bf), vmem((2, tok, cat_w), bf)]
        + [vmem((n_z, 2, N_FRAME, sub, 2 * block), bf), vmem((2, n_z, N_FRAME, sub, 2 * block), bf)]
        + [vmem((n_block, block, inner), f32)]
        + [vmem((n_z, block, inner), bf)] * 4
        + [vmem((block, inner), f32)] * 2
        + [dma((3,)), dma((4,)), dma((2,)), dma((2,)), dma((2,)), dma((2,)), dma, dma((n_z,)), dma, dma((n_z,)), dma, dma((n_z,))]
        + [dma((3,)), dma((3,)), dma((2, 2)), dma((3,)), dma((3,)), dma, dma, dma((2,)), dma, dma, dma((2,))]
        + [pltpu.SemaphoreType.REGULAR, pltpu.SemaphoreType.REGULAR((n_z,))]
    )
    grad_hidden, grad_w = pl.pallas_call(
        kernel,
        out_shape=(
            pltpu.VMEM((tok, width), bf),
            pltpu.VMEM((block, inner), f32),
        ),
        in_specs=[pl.BlockSpec(memory_space=pl.ANY)] * 6,
        out_specs=(pl.BlockSpec(memory_space=pltpu.VMEM),) * 2,
        scratch_shapes=scratch,
        compiler_params=pltpu.CompilerParams(
            collective_id=0, has_side_effects=True, vmem_limit_bytes=60 * 1024 * 1024
        ),
    )(*flat, hidden.reshape(tok, width), w_qkv)
    return grad_hidden.reshape(hidden.shape), grad_w


def solution(mesh):
    in_specs = (
        P("clip", "frame", None, None),
        P("clip", "frame", None, None),
        P("clip", "frame", None, None),
        P("clip", "frame", None, None),
        P("clip", "frame", None, None),
        P("frame", None),
    )
    out_specs = (P("clip", "frame", None, None), P("frame", None))
    fused = mesh.shape["clip"] == 2 and mesh.shape["frame"] == N_FRAME
    return jax.shard_map(
        per_device_fused if fused else per_device, mesh=mesh, in_specs=in_specs, out_specs=out_specs, check_vma=False
    )
```

```python
import functools
import math

import jax
import jax.numpy as jnp
from jax import lax
from jax.experimental import pallas as pl
from jax.experimental.pallas import tpu as pltpu
from jax.sharding import PartitionSpec as P

HDIM = 104


def attend_back(queries, keys, values, grad_out):
    score_scale = 1.0 / math.sqrt(HDIM)
    scores = (
        jnp.einsum("fpnd,gpnd->pnfg", queries, keys, preferred_element_type=jnp.float32)
        * score_scale
    )
    attn_probs = jax.nn.softmax(scores, axis=-1)
    probs_bf = attn_probs.astype(jnp.bfloat16)
    grad_v = jnp.einsum(
        "pnfg,fpnd->gpnd", probs_bf, grad_out, preferred_element_type=jnp.float32
    ).astype(jnp.bfloat16)
    grad_probs = jnp.einsum("fpnd,gpnd->pnfg", grad_out, values, preferred_element_type=jnp.float32)
    grad_scores = attn_probs * (
        grad_probs - jnp.sum(attn_probs * grad_probs, axis=-1, keepdims=True)
    )
    scores_bf = grad_scores.astype(jnp.bfloat16)
    grad_q = (
        jnp.einsum("pnfg,gpnd->fpnd", scores_bf, keys, preferred_element_type=jnp.float32)
        * score_scale
    ).astype(jnp.bfloat16)
    grad_k = (
        jnp.einsum("pnfg,fpnd->gpnd", scores_bf, queries, preferred_element_type=jnp.float32)
        * score_scale
    ).astype(jnp.bfloat16)
    return (grad_q, grad_k, grad_v)


def per_device(hidden, queries, keys, values, grad_attn, w_qkv):
    frames_local = hidden.shape[1]
    patches = hidden.shape[2]
    model_width = hidden.shape[3]
    inner_width = queries.shape[3]
    head_count = inner_width // HDIM
    row_count = frames_local * patches
    head_shape = (frames_local, patches, head_count, HDIM)
    q_local = queries.reshape(head_shape)
    k_local = keys.reshape(head_shape)
    v_local = values.reshape(head_shape)
    g_local = grad_attn.reshape(head_shape)
    q_patch, k_patch, v_patch, g_patch = (
        lax.all_to_all(q_local, "frame", split_axis=1, concat_axis=0, tiled=True),
        lax.all_to_all(k_local, "frame", split_axis=1, concat_axis=0, tiled=True),
        lax.all_to_all(v_local, "frame", split_axis=1, concat_axis=0, tiled=True),
        lax.all_to_all(g_local, "frame", split_axis=1, concat_axis=0, tiled=True),
    )
    grad_q, grad_k, grad_v = attend_back(q_patch, k_patch, v_patch, g_patch)
    grad_q, grad_k, grad_v = (
        lax.all_to_all(grad_q, "frame", split_axis=0, concat_axis=1, tiled=True),
        lax.all_to_all(grad_k, "frame", split_axis=0, concat_axis=1, tiled=True),
        lax.all_to_all(grad_v, "frame", split_axis=0, concat_axis=1, tiled=True),
    )
    value_rows = grad_v.reshape(row_count, inner_width)
    grad_cat = jnp.concatenate(
        [
            grad_q.reshape(row_count, inner_width),
            grad_k.reshape(row_count, inner_width),
            value_rows,
        ],
        axis=1,
    )
    grad_hid = lax.dot_general(
        grad_cat,
        lax.all_gather(w_qkv, "frame", axis=0, tiled=True),
        (((1,), (1,)), ((), ())),
        preferred_element_type=jnp.float32,
    )
    grad_hidden = grad_hid.astype(jnp.bfloat16).reshape(hidden.shape)
    hidden_rows = hidden.reshape(row_count, model_width)
    clip_count = lax.axis_size("clip")
    partial_grad = lax.psum_scatter(
        lax.dot_general(
            hidden_rows, value_rows, (((0,), (0,)), ((), ())), preferred_element_type=jnp.float32
        ),
        "frame",
        scatter_dimension=0,
        tiled=True,
    )
    grad_total = lax.psum(partial_grad, "clip")
    return (grad_hidden, grad_total / clip_count)


AX = {"z": (4, 4), "y": (2, 2), "x": (2, 1)}
N_FRAME = 16
ORDER = (
    "own_y", "own_z", "turn", "plane", "a00", "enter1", "a01", "enter2", "a02", "enter3", "a03",
    "a10", "a11", "a12", "a13", "hop1", "hidden", "spread", "y0", "attend0", "swap0", "attend1", "swap1",
    "hop2", "share0", "share1", "hop3", "y1", "y2", "y3", "weight", "project0", "project1", "project2",
    "project3", "sum_y", "sum_z", "finish", "collect",
)
NEAR = (1, 2, 0, 3)
COLS = ((0, 384), (384, 832))
PARTS = ((0, 512), (512, 832))
W_COLS = ((0, 1280), (1280, 2496))
W_CUT = 640


def move(f, axis, k):
    size, stride = AX[axis]
    digit = lax.rem(lax.div(f, stride), size)
    return f + (lax.rem(digit + k, size) - digit) * stride


def kernel(
    q_hbm, k_hbm, v_hbm, g_hbm, h_hbm, w_hbm,
    gh_ref, gw_ref,
    tq, tk, tv, tg, leaving, arrived,
    hb, hs, hall, w0, w1, acc_q, acc_k, acc_v, out_v, gall, cat, joined, ob, land,
    dws, y_s, y_r, z_s, z_r, fin_s, fin_r,
    loc, t_sem, a_send, a_recv, b_send, b_recv, wy_send, wy_recv, wz_send, wz_recv, wc_send, wc_recv,
    h_send, h_recv, x_sem, g_send, g_recv, o_send, o_recv, ry_sem, rz_send, rz_recv, f_sem, plane_sem, in_sem,
):
    c = lax.axis_index("clip")
    f = lax.axis_index("frame")
    other = 1 - c
    block = w_hbm.shape[0]
    tok = q_hbm.shape[1]
    sub = tok // N_FRAME
    n_block = w0.shape[0]
    n_z = AX["z"][0]
    last = n_z - 1
    scale = 1.0 / math.sqrt(HDIM)
    x = lax.rem(f, 2)
    pair = lax.div(f, 2)
    y = lax.rem(pair, 2)
    z = lax.div(pair, 2)
    beside = f + 1 - 2 * x
    across = move(f, "y", 1)
    slot = x * 2 + c

    def remote(src, dst, ss, rs, peer):
        pltpu.make_async_remote_copy(
            src_ref=src, dst_ref=dst, send_sem=ss, recv_sem=rs,
            device_id=peer, device_id_type=pl.DeviceIdType.MESH,
        ).start()

    def local(src, dst, sem):
        pltpu.make_async_copy(src, dst, sem).start()

    def wait(view, sem):
        pltpu.make_async_copy(view, view, sem).wait()

    def on_core(fn):
        for core in range(2):
            pl.when(c == core)(functools.partial(fn, core))

    barrier = pltpu.get_barrier_semaphore()

    def greet(peer):
        pl.semaphore_signal(barrier, inc=1, device_id=peer, device_id_type=pl.DeviceIdType.MESH)

    for peer in ((c, beside), (c, across), (other, f), (other, beside)):
        greet(peer)
    for way in (1, -1):

        @pl.when((z < last) if way == 1 else (z > 0))
        def _():
            greet((c, f + way * AX["z"][1]))

    turned = ((q_hbm, tq), (k_hbm, tk), (g_hbm, tg), (v_hbm, tv))
    pairs = [(leaving.at[i], arrived.at[i]) for i in range(4)]
    qb, kb, gb, vb = (arrived.at[i] for i in range(4))
    for i, (src, flat) in enumerate(turned):
        local(src, flat, t_sem.at[i])
    local(h_hbm, hb, loc.at[0])
    w_part = (w0, w1)
    for i in range(2):
        local(w_hbm.at[:, slice(*W_COLS[i])], w_part[i].at[pair], loc.at[1 + i])
    pl.semaphore_wait(barrier, 6 - jnp.where((z == 0) | (z == last), 1, 0))

    def tell(sem, peer):
        pl.semaphore_signal(sem, inc=1, device_id=peer, device_id_type=pl.DeviceIdType.MESH)

    def pass_in(from_z, way):
        @pl.when((z < last) if way == 1 else (z > 0))
        def _():
            tell(in_sem.at[from_z], (c, f + way * AX["z"][1]))

    def plane():
        tell(plane_sem, (c, across))
        pl.semaphore_wait(plane_sem, 1)
        for way in (1, -1):
            pass_in(z, way)

    def enter(h):
        for way in (1, -1):
            from_z = z - way * h

            @pl.when((from_z >= 0) & (from_z <= last))
            def _():
                pl.semaphore_wait(in_sem.at[from_z], 1)
                pass_in(from_z, way)

    def cut(core, k):
        return slice(0, W_CUT) if k == 0 else slice(W_CUT, w_part[core].shape[2])

    def w_at(core, zb, yb, k):
        return w_part[core].at[zb * 2 + yb, :, cut(core, k)]

    def w_wait(core, k, sem):
        wait(w_part[core].at[0, :, cut(core, k)], sem)

    def forward(core, zb, yb, k):
        view = w_at(core, zb, yb, k)
        remote(view, view, wc_send, wc_recv.at[zb], (other, f))

    def pass_y(core, zb, k, src=None):
        dst = w_at(core, zb, y, k)
        remote(dst if src is None else src, dst, wy_send, wy_recv.at[zb, k], (c, across))

    def climb(core, zb, way, k, src=None):
        dst = w_at(core, zb, y, k)

        @pl.when((z < last) if way == 1 else (z > 0))
        def _():
            peer = (c, f + way * AX["z"][1])
            remote(dst if src is None else src, dst, wz_send, wz_recv.at[zb, k], peer)

    def own(core, k):
        low, high = W_COLS[core]
        return w_hbm.at[:, (slice(low, low + W_CUT) if k == 0 else slice(low + W_CUT, high))]

    def w_start_y(core):
        for k in range(2):
            pass_y(core, z, k, own(core, k))

    def w_start_z(core):
        for k in range(2):
            for way in (1, -1):
                climb(core, z, way, k, own(core, k))

    def w_hop(h, core):
        for k in range(2):
            for way in (1, -1):
                from_z = z - way * h

                @pl.when((from_z >= 0) & (from_z <= last))
                def _():
                    w_wait(core, k, wz_recv.at[from_z, k])
                    climb(core, from_z, way, k)
                    pass_y(core, from_z, k)
                    forward(core, from_z, y, k)

    def w_y0(core):
        for k in range(2):
            w_wait(core, k, wy_recv.at[z, k])
            forward(core, z, 1 - y, k)

    def by_distance(j):
        at_end = (z == 0) | (z == last)
        up = jnp.where(at_end, j, NEAR[j])
        return jnp.where(z * 2 < n_z, up, last - up)

    def w_ys(j, core):
        zb = by_distance(j)
        for k in range(2):
            w_wait(core, k, wy_recv.at[zb, k])
            forward(core, zb, 1 - y, k)

    def w_drain(core):
        wait(w_part[core].at[pl.ds(0, n_z)], wy_send)
        edge = (z == 0) | (z == last)
        for ends, count in ((True, 1), (False, 5)):

            @pl.when(edge if ends else jnp.logical_not(edge))
            def _():
                wait(w_part[core].at[pl.ds(0, count)], wz_send)

        wait(w_part[core].at[pl.ds(0, n_block - 1)], wc_send)

    def turn():
        for i, (src, _) in enumerate(pairs):
            pltpu.make_async_copy(turned[i][0], turned[i][1], t_sem.at[i]).wait()
            src[...] = turned[i][1][...].T.reshape(src.shape)

    def exchange(part, h):
        cols = slice(*PARTS[part])

        def to_frame(to):
            for src, dst in pairs:
                remote(src.at[to, :, cols], dst.at[f, :, cols], a_send.at[part], a_recv.at[part], (c, to))

        if h == 0:
            for src, dst in pairs:
                local(src.at[f, :, cols], dst.at[f, :, cols], a_recv.at[part])
            for to in (beside, across, move(across, "x", 1)):
                to_frame(to)
            return
        for way in (1, -1):
            to_z = z - way * h

            @pl.when((to_z >= 0) & (to_z <= last))
            def _():
                @pl.loop(0, AX["z"][1])
                def _(k):
                    to_frame(to_z * AX["z"][1] + k)

    acc_q[...] = jnp.zeros_like(acc_q)
    acc_k[...] = jnp.zeros_like(acc_k)
    acc_v[...] = jnp.zeros_like(acc_v)
    row_id = lax.broadcasted_iota(jnp.int32, (tok, tok), 0)
    col_id = lax.broadcasted_iota(jnp.int32, (tok, tok), 1)
    same = lax.rem(row_id, sub) == lax.rem(col_id, sub)

    width_all = q_hbm.shape[0]
    heads = width_all // HDIM
    nt = (((1,), (1,)), ((), ()))
    tn = (((0,), (0,)), ((), ()))
    nn = (((1,), (0,)), ((), ()))
    dot = functools.partial(lax.dot_general, preferred_element_type=jnp.float32)

    def window(n):
        low = n * HDIM // 128 * 128
        high = min(-(-(n + 1) * HDIM // 128) * 128, width_all)
        lane = lax.broadcasted_iota(jnp.int32, (tok, high - low), 1) + low
        keep = jnp.where((lane >= n * HDIM) & (lane < (n + 1) * HDIM), 1.0, 0.0)
        return slice(low, high), keep.astype(jnp.bfloat16)

    def rows(ref, win):
        return ref[:, :, win].reshape(tok, win.stop - win.start)

    def hidden():
        pltpu.make_async_copy(h_hbm, hb, loc.at[0]).wait()
        for k in range(2):
            half = jnp.concatenate(
                [hb[:, (2 * i + k) * block : (2 * i + k + 1) * block] for i in range(n_block)], axis=1
            )
            hs[k] = half
        hall[slot] = hs[x]
        remote(hs.at[1 - x], hall.at[slot], h_send.at[0], h_recv.at[0], (c, beside))
        remote(hs.at[x], hall.at[slot], h_send.at[1], h_recv.at[1], (other, f))

    def spread():
        theirs = hall.at[(1 - x) * 2 + c]
        wait(theirs, h_recv.at[0])
        remote(theirs, theirs, h_send.at[2], h_recv.at[2], (other, f))

    def attend(part):
        wait(arrived.at[:, :, :, slice(*PARTS[part])], a_recv.at[part])
        half = heads // 2
        for n in range(part * half, (part + 1) * half):
            win, keep = window(n)
            g = rows(gb, win) * keep
            s = dot(rows(qb, win) * keep, rows(kb, win), nt) * scale
            s = jnp.where(same, s, -1e30)
            e = jnp.exp(s - jnp.max(s, axis=1, keepdims=True))
            p = e / jnp.sum(e, axis=1, keepdims=True)
            acc_v[:, win] += dot(p.astype(jnp.bfloat16), g, tn)
            dp = dot(g, rows(vb, win), nt)
            ds = (p * (dp - jnp.sum(p * dp, axis=1, keepdims=True))).astype(jnp.bfloat16)
            acc_q[:, win] += dot(ds, rows(kb, win) * keep, nn)
            acc_k[:, win] += dot(ds, rows(qb, win) * keep, tn)
        cols = slice(*COLS[part])
        grad_v = acc_v[:, cols].astype(jnp.bfloat16)
        out_v[:, :, cols] = grad_v.reshape(N_FRAME, sub, cols.stop - cols.start)
        local(out_v.at[f, :, cols], gall.at[slot, f, :, cols], b_recv.at[part])

        @pl.loop(1, N_FRAME)
        def _(d):
            to = lax.rem(f + d, N_FRAME)
            dst = gall.at[lax.rem(to, 2) * 2 + c, f, :, cols]
            remote(out_v.at[to, :, cols], dst, b_send.at[part], b_recv.at[part], (c, to))

        cat[x, 0, :, cols] = (acc_q[:, cols] * scale).astype(jnp.bfloat16)
        cat[x, 1, :, cols] = (acc_k[:, cols] * scale).astype(jnp.bfloat16)
        cat[x, 2, :, cols] = grad_v

    def swap(part):
        mine = cat.at[x, :, :, slice(*COLS[part])]
        remote(mine, mine, x_sem.at[0, part], x_sem.at[1, part], (c, beside))

    def share(to, core):
        wait(gall.at[0, :, :, slice(*COLS[to])], b_recv.at[to])
        src = gall.at[slot, :, :, slice(*COLS[to])]
        remote(src, src, g_send.at[to], g_recv.at[0 if to == core else 1], (to, beside))
        if to != core:
            remote(src, src, g_send.at[2], g_recv.at[2], (to, f))

    def weight(core):
        cols = slice(*COLS[core])
        wait(hall.at[0], h_recv.at[1])
        wait(hall.at[0], h_recv.at[2])
        for i in range(3):
            wait(gall.at[0, :, :, cols], g_recv.at[i])
        n = cols.stop - cols.start
        total = dot(hall[...].reshape(4 * tok, hall.shape[2]), gall[:, :, :, cols].reshape(4 * tok, n), tn)
        dws[:, :, cols] = total.reshape(n_block, block, n)
        for zb in range(n_z):
            y_s[zb, :, cols] = dws[zb * 2 + 1 - y, :, cols].astype(jnp.bfloat16)
        remote(y_s.at[:, :, cols], y_r.at[:, :, cols], ry_sem.at[0], ry_sem.at[1], (c, across))

    def sum_y(core):
        cols = slice(*COLS[core])
        wait(y_r.at[:, :, cols], ry_sem.at[1])
        for k in range(1, n_z):
            zb = lax.rem(z + k, n_z)
            total = dws[zb * 2 + y, :, cols] + y_r[zb, :, cols].astype(jnp.float32)
            z_s[zb, :, cols] = total.astype(jnp.bfloat16)
            remote(z_s.at[zb, :, cols], z_r.at[z, :, cols], rz_send, rz_recv, (c, move(f, "z", k)))
        dws[pair, :, cols] += y_r[z, :, cols].astype(jnp.float32)

    def sum_z(core):
        cols = slice(*COLS[core])
        wait(z_r.at[pl.ds(0, n_z - 1), :, cols], rz_recv)
        total = dws[pair, :, cols]
        for k in range(1, n_z):
            total += z_r[lax.rem(z + k, n_z), :, cols].astype(jnp.float32)
        total *= 0.5
        fin_s[:, cols] = total
        remote(fin_s.at[:, cols], fin_r.at[:, cols], f_sem.at[0], f_sem.at[1], (other, f))
        gw_ref[:, cols] = total

    def finish(core):
        mine, rest = slice(*COLS[core]), slice(*COLS[1 - core])
        wait(fin_r.at[:, rest], f_sem.at[1])
        gw_ref[:, rest] = fin_r[:, rest]
        wait(fin_s.at[:, mine], f_sem.at[0])
        wait(y_s.at[:, :, mine], ry_sem.at[0])
        wait(z_s.at[pl.ds(0, n_z - 1), :, mine], rz_send)
        for to in range(2):
            wait(gall.at[0, :, :, slice(*COLS[to])], g_send.at[to])
            if to != core:
                wait(gall.at[0, :, :, slice(*COLS[to])], g_send.at[2])
        w_drain(core)

    def project(j):
        zb = by_distance(j)
        if j == 0:
            for i in range(2):
                wait(cat.at[0, :, :, slice(*COLS[i])], x_sem.at[1, i])
                pltpu.make_async_copy(w_hbm.at[:, slice(*W_COLS[i])], w_part[i].at[pair], loc.at[1 + i]).wait()
        on_core(lambda core: wait(w_part[1 - core].at[pl.ds(0, 2 if j else 1)], wc_recv.at[zb]))
        if j == 0:
            for k in range(2):
                joined[k] = jnp.concatenate([cat[k, i] for i in range(3)], axis=1)
        grads = joined[...].reshape(2 * tok, joined.shape[2])
        parts = [w[pl.ds(zb * 2, 2)].reshape(2 * block, w.shape[2]) for w in w_part]
        res = sum(dot(grads[:, slice(*W_COLS[i])], parts[i], nt) for i in range(2))
        ob[zb] = res.astype(jnp.bfloat16).reshape(2, N_FRAME, sub, 2 * block)
        dst = land.at[x, zb, pl.ds(pair * 2, 2)]
        local(ob.at[zb, :, f], dst, o_recv)

        @pl.loop(1, N_FRAME)
        def _(d):
            to = lax.rem(f + d, N_FRAME)
            remote(ob.at[zb, :, to], dst, o_send, o_recv, (c, to))

    def collect():
        wait(land, o_recv)
        pieces = [
            land[k, zb][:, :, yb * block : (yb + 1) * block].reshape(tok, block)
            for zb in range(n_z) for yb in range(2) for k in range(2)
        ]
        gh_ref[...] = jnp.concatenate(pieces, axis=1)

    steps = {
        "hidden": hidden, "spread": spread, "turn": turn, "plane": plane,
        "collect": collect,
    }
    for i in range(2):
        for h in range(n_z):
            steps["a" + str(i) + str(h)] = functools.partial(exchange, i, h)
        steps["swap" + str(i)] = functools.partial(swap, i)
        steps["attend" + str(i)] = functools.partial(attend, i)
        steps["share" + str(i)] = functools.partial(on_core, functools.partial(share, i))
    for name, fn in (
        ("own_y", w_start_y), ("own_z", w_start_z), ("y0", w_y0), ("ys", w_ys), ("weight", weight), ("sum_y", sum_y),
        ("sum_z", sum_z), ("finish", finish),
    ):
        steps[name] = functools.partial(on_core, fn)
    for i in range(1, n_z):
        steps["hop" + str(i)] = functools.partial(on_core, functools.partial(w_hop, i))
        steps["enter" + str(i)] = functools.partial(enter, i)
        steps["y" + str(i)] = functools.partial(on_core, functools.partial(w_ys, i))
    for j in range(n_z):
        steps["project" + str(j)] = functools.partial(project, j)
    for name in ORDER:
        steps[name]()

    for i in range(2):
        wait(leaving.at[:, pl.ds(0, N_FRAME - 1), :, slice(*PARTS[i])], a_send.at[i])
        wait(out_v.at[pl.ds(0, N_FRAME - 1), :, slice(*COLS[i])], b_send.at[i])
        wait(cat.at[0, :, :, slice(*COLS[i])], x_sem.at[0, i])
    wait(ob.at[:, :, pl.ds(0, N_FRAME - 1)], o_send)
    for i in range(3):
        wait(hs.at[0], h_send.at[i])


def per_device_fused(hidden, queries, keys, values, grad_attn, w_qkv):
    tok, width = hidden.shape[2], hidden.shape[3]
    inner = queries.shape[3]
    block, cat_w = w_qkv.shape
    flat = [
        jnp.swapaxes(a.reshape(tok, inner), 0, 1) for a in (queries, keys, values, grad_attn)
    ]
    bf, f32 = jnp.bfloat16, jnp.float32
    dma = pltpu.SemaphoreType.DMA
    sub, n_block, half = tok // N_FRAME, N_FRAME // 2, width // 2
    n_z = AX["z"][0]
    vmem = pltpu.VMEM
    scratch = (
        [vmem((inner, tok), bf)] * 4
        + [vmem((4, N_FRAME, sub, inner), bf)] * 2
        + [vmem((tok, width), bf), vmem((2, tok, half), bf), vmem((4, tok, half), bf)]
        + [vmem((n_block, block, high - low), bf) for low, high in W_COLS]
        + [vmem((tok, inner), f32)] * 3
        + [vmem((N_FRAME, sub, inner), bf), vmem((4, N_FRAME, sub, inner), bf)]
        + [vmem((2, 3, tok, inner), bf), vmem((2, tok, cat_w), bf)]
        + [vmem((n_z, 2, N_FRAME, sub, 2 * block), bf), vmem((2, n_z, N_FRAME, sub, 2 * block), bf)]
        + [vmem((n_block, block, inner), f32)]
        + [vmem((n_z, block, inner), bf)] * 4
        + [vmem((block, inner), f32)] * 2
        + [dma((3,)), dma((4,)), dma((2,)), dma((2,)), dma((2,)), dma((2,)), dma, dma((n_z, 2)), dma, dma((n_z, 2)), dma, dma((n_z,))]
        + [dma((3,)), dma((3,)), dma((2, 2)), dma((3,)), dma((3,)), dma, dma, dma((2,)), dma, dma, dma((2,))]
        + [pltpu.SemaphoreType.REGULAR, pltpu.SemaphoreType.REGULAR((n_z,))]
    )
    grad_hidden, grad_w = pl.pallas_call(
        kernel,
        out_shape=(
            pltpu.VMEM((tok, width), bf),
            pltpu.VMEM((block, inner), f32),
        ),
        in_specs=[pl.BlockSpec(memory_space=pl.ANY)] * 6,
        out_specs=(pl.BlockSpec(memory_space=pltpu.VMEM),) * 2,
        scratch_shapes=scratch,
        compiler_params=pltpu.CompilerParams(
            collective_id=0, has_side_effects=True, vmem_limit_bytes=60 * 1024 * 1024
        ),
    )(*flat, hidden.reshape(tok, width), w_qkv)
    return grad_hidden.reshape(hidden.shape), grad_w


def solution(mesh):
    in_specs = (
        P("clip", "frame", None, None),
        P("clip", "frame", None, None),
        P("clip", "frame", None, None),
        P("clip", "frame", None, None),
        P("clip", "frame", None, None),
        P("frame", None),
    )
    out_specs = (P("clip", "frame", None, None), P("frame", None))
    fused = mesh.shape["clip"] == 2 and mesh.shape["frame"] == N_FRAME
    return jax.shard_map(
        per_device_fused if fused else per_device, mesh=mesh, in_specs=in_specs, out_specs=out_specs, check_vma=False
    )
```

```python
import functools
import math

import jax
import jax.numpy as jnp
from jax import lax
from jax.experimental import pallas as pl
from jax.experimental.pallas import tpu as pltpu
from jax.sharding import PartitionSpec as P

HDIM = 104


def attend_back(queries, keys, values, grad_out):
    score_scale = 1.0 / math.sqrt(HDIM)
    scores = (
        jnp.einsum("fpnd,gpnd->pnfg", queries, keys, preferred_element_type=jnp.float32)
        * score_scale
    )
    attn_probs = jax.nn.softmax(scores, axis=-1)
    probs_bf = attn_probs.astype(jnp.bfloat16)
    grad_v = jnp.einsum(
        "pnfg,fpnd->gpnd", probs_bf, grad_out, preferred_element_type=jnp.float32
    ).astype(jnp.bfloat16)
    grad_probs = jnp.einsum("fpnd,gpnd->pnfg", grad_out, values, preferred_element_type=jnp.float32)
    grad_scores = attn_probs * (
        grad_probs - jnp.sum(attn_probs * grad_probs, axis=-1, keepdims=True)
    )
    scores_bf = grad_scores.astype(jnp.bfloat16)
    grad_q = (
        jnp.einsum("pnfg,gpnd->fpnd", scores_bf, keys, preferred_element_type=jnp.float32)
        * score_scale
    ).astype(jnp.bfloat16)
    grad_k = (
        jnp.einsum("pnfg,fpnd->gpnd", scores_bf, queries, preferred_element_type=jnp.float32)
        * score_scale
    ).astype(jnp.bfloat16)
    return (grad_q, grad_k, grad_v)


def per_device(hidden, queries, keys, values, grad_attn, w_qkv):
    frames_local = hidden.shape[1]
    patches = hidden.shape[2]
    model_width = hidden.shape[3]
    inner_width = queries.shape[3]
    head_count = inner_width // HDIM
    row_count = frames_local * patches
    head_shape = (frames_local, patches, head_count, HDIM)
    q_local = queries.reshape(head_shape)
    k_local = keys.reshape(head_shape)
    v_local = values.reshape(head_shape)
    g_local = grad_attn.reshape(head_shape)
    q_patch, k_patch, v_patch, g_patch = (
        lax.all_to_all(q_local, "frame", split_axis=1, concat_axis=0, tiled=True),
        lax.all_to_all(k_local, "frame", split_axis=1, concat_axis=0, tiled=True),
        lax.all_to_all(v_local, "frame", split_axis=1, concat_axis=0, tiled=True),
        lax.all_to_all(g_local, "frame", split_axis=1, concat_axis=0, tiled=True),
    )
    grad_q, grad_k, grad_v = attend_back(q_patch, k_patch, v_patch, g_patch)
    grad_q, grad_k, grad_v = (
        lax.all_to_all(grad_q, "frame", split_axis=0, concat_axis=1, tiled=True),
        lax.all_to_all(grad_k, "frame", split_axis=0, concat_axis=1, tiled=True),
        lax.all_to_all(grad_v, "frame", split_axis=0, concat_axis=1, tiled=True),
    )
    value_rows = grad_v.reshape(row_count, inner_width)
    grad_cat = jnp.concatenate(
        [
            grad_q.reshape(row_count, inner_width),
            grad_k.reshape(row_count, inner_width),
            value_rows,
        ],
        axis=1,
    )
    grad_hid = lax.dot_general(
        grad_cat,
        lax.all_gather(w_qkv, "frame", axis=0, tiled=True),
        (((1,), (1,)), ((), ())),
        preferred_element_type=jnp.float32,
    )
    grad_hidden = grad_hid.astype(jnp.bfloat16).reshape(hidden.shape)
    hidden_rows = hidden.reshape(row_count, model_width)
    clip_count = lax.axis_size("clip")
    partial_grad = lax.psum_scatter(
        lax.dot_general(
            hidden_rows, value_rows, (((0,), (0,)), ((), ())), preferred_element_type=jnp.float32
        ),
        "frame",
        scatter_dimension=0,
        tiled=True,
    )
    grad_total = lax.psum(partial_grad, "clip")
    return (grad_hidden, grad_total / clip_count)


AX = {"z": (4, 4), "y": (2, 2), "x": (2, 1)}
N_FRAME = 16
ORDER = (
    "own_y", "own_z", "turn", "plane", "a00", "enter1", "a01", "enter2", "a02", "enter3", "a03",
    "a10", "a11", "a12", "a13", "hop1", "hidden", "spread", "y0", "attend0", "swap0", "attend1", "swap1",
    "hop2", "share0", "share1", "hop3", "y1", "y2", "y3", "weight", "project0", "project1", "project2",
    "project3", "sum_y", "collect", "sum_z", "finish",
)
NEAR = (1, 2, 0, 3)
COLS = ((0, 384), (384, 832))
PARTS = ((0, 512), (512, 832))
W_COLS = ((0, 1280), (1280, 2496))
W_CUT = 640


def move(f, axis, k):
    size, stride = AX[axis]
    digit = lax.rem(lax.div(f, stride), size)
    return f + (lax.rem(digit + k, size) - digit) * stride


def kernel(
    q_hbm, k_hbm, v_hbm, g_hbm, h_hbm, w_hbm,
    gh_ref, gw_ref,
    tq, tk, tv, tg, leaving, arrived,
    hb, hs, hall, w0, w1, acc_q, acc_k, acc_v, out_v, gall, cat, joined, ob, land,
    dws, y_s, y_r, z_s, z_r, fin_s, fin_r,
    loc, t_sem, a_send, a_recv, b_send, b_recv, wy_send, wy_recv, wz_send, wz_recv, wc_send, wc_recv,
    h_send, h_recv, x_sem, g_send, g_recv, o_send, o_recv, ry_sem, rz_send, rz_recv, f_sem, plane_sem, in_sem,
):
    c = lax.axis_index("clip")
    f = lax.axis_index("frame")
    other = 1 - c
    block = w_hbm.shape[0]
    tok = q_hbm.shape[1]
    sub = tok // N_FRAME
    n_block = w0.shape[0]
    n_z = AX["z"][0]
    last = n_z - 1
    scale = 1.0 / math.sqrt(HDIM)
    x = lax.rem(f, 2)
    pair = lax.div(f, 2)
    y = lax.rem(pair, 2)
    z = lax.div(pair, 2)
    beside = f + 1 - 2 * x
    across = move(f, "y", 1)
    slot = x * 2 + c

    def remote(src, dst, ss, rs, peer):
        pltpu.make_async_remote_copy(
            src_ref=src, dst_ref=dst, send_sem=ss, recv_sem=rs,
            device_id=peer, device_id_type=pl.DeviceIdType.MESH,
        ).start()

    def local(src, dst, sem):
        pltpu.make_async_copy(src, dst, sem).start()

    def wait(view, sem):
        pltpu.make_async_copy(view, view, sem).wait()

    def on_core(fn):
        for core in range(2):
            pl.when(c == core)(functools.partial(fn, core))

    barrier = pltpu.get_barrier_semaphore()

    def greet(peer):
        pl.semaphore_signal(barrier, inc=1, device_id=peer, device_id_type=pl.DeviceIdType.MESH)

    for peer in ((c, beside), (c, across), (other, f), (other, beside)):
        greet(peer)
    for way in (1, -1):

        @pl.when((z < last) if way == 1 else (z > 0))
        def _():
            greet((c, f + way * AX["z"][1]))

    turned = ((q_hbm, tq), (k_hbm, tk), (g_hbm, tg), (v_hbm, tv))
    pairs = [(leaving.at[i], arrived.at[i]) for i in range(4)]
    qb, kb, gb, vb = (arrived.at[i] for i in range(4))
    for i, (src, flat) in enumerate(turned):
        local(src, flat, t_sem.at[i])
    local(h_hbm, hb, loc.at[0])
    w_part = (w0, w1)
    for i in range(2):
        local(w_hbm.at[:, slice(*W_COLS[i])], w_part[i].at[pair], loc.at[1 + i])
    pl.semaphore_wait(barrier, 6 - jnp.where((z == 0) | (z == last), 1, 0))

    def tell(sem, peer):
        pl.semaphore_signal(sem, inc=1, device_id=peer, device_id_type=pl.DeviceIdType.MESH)

    def pass_in(from_z, way):
        @pl.when((z < last) if way == 1 else (z > 0))
        def _():
            tell(in_sem.at[from_z], (c, f + way * AX["z"][1]))

    def plane():
        tell(plane_sem, (c, across))
        pl.semaphore_wait(plane_sem, 1)
        for way in (1, -1):
            pass_in(z, way)

    def enter(h):
        for way in (1, -1):
            from_z = z - way * h

            @pl.when((from_z >= 0) & (from_z <= last))
            def _():
                pl.semaphore_wait(in_sem.at[from_z], 1)
                pass_in(from_z, way)

    def cut(core, k):
        return slice(0, W_CUT) if k == 0 else slice(W_CUT, w_part[core].shape[2])

    def w_at(core, zb, yb, k):
        return w_part[core].at[zb * 2 + yb, :, cut(core, k)]

    def w_wait(core, k, sem):
        wait(w_part[core].at[0, :, cut(core, k)], sem)

    def forward(core, zb, yb, k):
        view = w_at(core, zb, yb, k)
        remote(view, view, wc_send, wc_recv.at[zb], (other, f))

    def pass_y(core, zb, k, src=None):
        dst = w_at(core, zb, y, k)
        remote(dst if src is None else src, dst, wy_send, wy_recv.at[zb, k], (c, across))

    def climb(core, zb, way, k, src=None):
        dst = w_at(core, zb, y, k)

        @pl.when((z < last) if way == 1 else (z > 0))
        def _():
            peer = (c, f + way * AX["z"][1])
            remote(dst if src is None else src, dst, wz_send, wz_recv.at[zb, k], peer)

    def own(core, k):
        low, high = W_COLS[core]
        return w_hbm.at[:, (slice(low, low + W_CUT) if k == 0 else slice(low + W_CUT, high))]

    def w_start_y(core):
        for k in range(2):
            pass_y(core, z, k, own(core, k))

    def w_start_z(core):
        for k in range(2):
            for way in (1, -1):
                climb(core, z, way, k, own(core, k))

    def w_hop(h, core):
        for k in range(2):
            for way in (1, -1):
                from_z = z - way * h

                @pl.when((from_z >= 0) & (from_z <= last))
                def _():
                    w_wait(core, k, wz_recv.at[from_z, k])
                    climb(core, from_z, way, k)
                    pass_y(core, from_z, k)
                    forward(core, from_z, y, k)

    def w_y0(core):
        for k in range(2):
            w_wait(core, k, wy_recv.at[z, k])
            forward(core, z, 1 - y, k)

    def by_distance(j):
        at_end = (z == 0) | (z == last)
        up = jnp.where(at_end, j, NEAR[j])
        return jnp.where(z * 2 < n_z, up, last - up)

    def w_ys(j, core):
        zb = by_distance(j)
        for k in range(2):
            w_wait(core, k, wy_recv.at[zb, k])
            forward(core, zb, 1 - y, k)

    def w_drain(core):
        wait(w_part[core].at[pl.ds(0, n_z)], wy_send)
        edge = (z == 0) | (z == last)
        for ends, count in ((True, 1), (False, 5)):

            @pl.when(edge if ends else jnp.logical_not(edge))
            def _():
                wait(w_part[core].at[pl.ds(0, count)], wz_send)

        wait(w_part[core].at[pl.ds(0, n_block - 1)], wc_send)

    def turn():
        for i, (src, _) in enumerate(pairs):
            pltpu.make_async_copy(turned[i][0], turned[i][1], t_sem.at[i]).wait()
            src[...] = turned[i][1][...].T.reshape(src.shape)

    def exchange(part, h):
        cols = slice(*PARTS[part])

        def to_frame(to):
            for src, dst in pairs:
                remote(src.at[to, :, cols], dst.at[f, :, cols], a_send.at[part], a_recv.at[part], (c, to))

        if h == 0:
            for src, dst in pairs:
                local(src.at[f, :, cols], dst.at[f, :, cols], a_recv.at[part])
            for to in (beside, across, move(across, "x", 1)):
                to_frame(to)
            return
        for way in (1, -1):
            to_z = z - way * h

            @pl.when((to_z >= 0) & (to_z <= last))
            def _():
                @pl.loop(0, AX["z"][1])
                def _(k):
                    to_frame(to_z * AX["z"][1] + k)

    acc_q[...] = jnp.zeros_like(acc_q)
    acc_k[...] = jnp.zeros_like(acc_k)
    acc_v[...] = jnp.zeros_like(acc_v)
    row_id = lax.broadcasted_iota(jnp.int32, (tok, tok), 0)
    col_id = lax.broadcasted_iota(jnp.int32, (tok, tok), 1)
    same = lax.rem(row_id, sub) == lax.rem(col_id, sub)

    width_all = q_hbm.shape[0]
    heads = width_all // HDIM
    nt = (((1,), (1,)), ((), ()))
    tn = (((0,), (0,)), ((), ()))
    nn = (((1,), (0,)), ((), ()))
    dot = functools.partial(lax.dot_general, preferred_element_type=jnp.float32)

    def window(n):
        low = n * HDIM // 128 * 128
        high = min(-(-(n + 1) * HDIM // 128) * 128, width_all)
        lane = lax.broadcasted_iota(jnp.int32, (tok, high - low), 1) + low
        keep = jnp.where((lane >= n * HDIM) & (lane < (n + 1) * HDIM), 1.0, 0.0)
        return slice(low, high), keep.astype(jnp.bfloat16)

    def rows(ref, win):
        return ref[:, :, win].reshape(tok, win.stop - win.start)

    def hidden():
        pltpu.make_async_copy(h_hbm, hb, loc.at[0]).wait()
        for k in range(2):
            half = jnp.concatenate(
                [hb[:, (2 * i + k) * block : (2 * i + k + 1) * block] for i in range(n_block)], axis=1
            )
            hs[k] = half
        hall[slot] = hs[x]
        remote(hs.at[1 - x], hall.at[slot], h_send.at[0], h_recv.at[0], (c, beside))
        remote(hs.at[x], hall.at[slot], h_send.at[1], h_recv.at[1], (other, f))

    def spread():
        theirs = hall.at[(1 - x) * 2 + c]
        wait(theirs, h_recv.at[0])
        remote(theirs, theirs, h_send.at[2], h_recv.at[2], (other, f))

    def attend(part):
        wait(arrived.at[:, :, :, slice(*PARTS[part])], a_recv.at[part])
        half = heads // 2
        for n in range(part * half, (part + 1) * half):
            win, keep = window(n)
            g = rows(gb, win) * keep
            s = dot(rows(qb, win) * keep, rows(kb, win), nt) * scale
            s = jnp.where(same, s, -1e30)
            e = jnp.exp(s - jnp.max(s, axis=1, keepdims=True))
            p = e / jnp.sum(e, axis=1, keepdims=True)
            acc_v[:, win] += dot(p.astype(jnp.bfloat16), g, tn)
            dp = dot(g, rows(vb, win), nt)
            ds = (p * (dp - jnp.sum(p * dp, axis=1, keepdims=True))).astype(jnp.bfloat16)
            acc_q[:, win] += dot(ds, rows(kb, win) * keep, nn)
            acc_k[:, win] += dot(ds, rows(qb, win) * keep, tn)
        cols = slice(*COLS[part])
        grad_v = acc_v[:, cols].astype(jnp.bfloat16)
        out_v[:, :, cols] = grad_v.reshape(N_FRAME, sub, cols.stop - cols.start)
        local(out_v.at[f, :, cols], gall.at[slot, f, :, cols], b_recv.at[part])

        @pl.loop(1, N_FRAME)
        def _(d):
            to = lax.rem(f + d, N_FRAME)
            dst = gall.at[lax.rem(to, 2) * 2 + c, f, :, cols]
            remote(out_v.at[to, :, cols], dst, b_send.at[part], b_recv.at[part], (c, to))

        cat[x, 0, :, cols] = (acc_q[:, cols] * scale).astype(jnp.bfloat16)
        cat[x, 1, :, cols] = (acc_k[:, cols] * scale).astype(jnp.bfloat16)
        cat[x, 2, :, cols] = grad_v

    def swap(part):
        mine = cat.at[x, :, :, slice(*COLS[part])]
        remote(mine, mine, x_sem.at[0, part], x_sem.at[1, part], (c, beside))

    def share(to, core):
        wait(gall.at[0, :, :, slice(*COLS[to])], b_recv.at[to])
        src = gall.at[slot, :, :, slice(*COLS[to])]
        remote(src, src, g_send.at[to], g_recv.at[0 if to == core else 1], (to, beside))
        if to != core:
            remote(src, src, g_send.at[2], g_recv.at[2], (to, f))

    def weight(core):
        cols = slice(*COLS[core])
        wait(hall.at[0], h_recv.at[1])
        wait(hall.at[0], h_recv.at[2])
        for i in range(3):
            wait(gall.at[0, :, :, cols], g_recv.at[i])
        n = cols.stop - cols.start
        total = dot(hall[...].reshape(4 * tok, hall.shape[2]), gall[:, :, :, cols].reshape(4 * tok, n), tn)
        dws[:, :, cols] = total.reshape(n_block, block, n)
        for zb in range(n_z):
            y_s[zb, :, cols] = dws[zb * 2 + 1 - y, :, cols].astype(jnp.bfloat16)
        remote(y_s.at[:, :, cols], y_r.at[:, :, cols], ry_sem.at[0], ry_sem.at[1], (c, across))

    def sum_y(core):
        cols = slice(*COLS[core])
        wait(y_r.at[:, :, cols], ry_sem.at[1])
        for k in range(1, n_z):
            zb = lax.rem(z + k, n_z)
            total = dws[zb * 2 + y, :, cols] + y_r[zb, :, cols].astype(jnp.float32)
            z_s[zb, :, cols] = total.astype(jnp.bfloat16)
            remote(z_s.at[zb, :, cols], z_r.at[z, :, cols], rz_send, rz_recv, (c, move(f, "z", k)))
        dws[pair, :, cols] += y_r[z, :, cols].astype(jnp.float32)

    def sum_z(core):
        cols = slice(*COLS[core])
        wait(z_r.at[pl.ds(0, n_z - 1), :, cols], rz_recv)
        total = dws[pair, :, cols]
        for k in range(1, n_z):
            total += z_r[lax.rem(z + k, n_z), :, cols].astype(jnp.float32)
        total *= 0.5
        fin_s[:, cols] = total
        remote(fin_s.at[:, cols], fin_r.at[:, cols], f_sem.at[0], f_sem.at[1], (other, f))
        gw_ref[:, cols] = total

    def finish(core):
        mine, rest = slice(*COLS[core]), slice(*COLS[1 - core])
        wait(fin_r.at[:, rest], f_sem.at[1])
        gw_ref[:, rest] = fin_r[:, rest]
        wait(fin_s.at[:, mine], f_sem.at[0])
        wait(y_s.at[:, :, mine], ry_sem.at[0])
        wait(z_s.at[pl.ds(0, n_z - 1), :, mine], rz_send)
        for to in range(2):
            wait(gall.at[0, :, :, slice(*COLS[to])], g_send.at[to])
            if to != core:
                wait(gall.at[0, :, :, slice(*COLS[to])], g_send.at[2])
        w_drain(core)

    def project(j):
        zb = by_distance(j)
        if j == 0:
            for i in range(2):
                wait(cat.at[0, :, :, slice(*COLS[i])], x_sem.at[1, i])
                pltpu.make_async_copy(w_hbm.at[:, slice(*W_COLS[i])], w_part[i].at[pair], loc.at[1 + i]).wait()
        on_core(lambda core: wait(w_part[1 - core].at[pl.ds(0, 2 if j else 1)], wc_recv.at[zb]))
        if j == 0:
            for k in range(2):
                joined[k] = jnp.concatenate([cat[k, i] for i in range(3)], axis=1)
        grads = joined[...].reshape(2 * tok, joined.shape[2])
        parts = [w[pl.ds(zb * 2, 2)].reshape(2 * block, w.shape[2]) for w in w_part]
        res = sum(dot(grads[:, slice(*W_COLS[i])], parts[i], nt) for i in range(2))
        ob[zb] = res.astype(jnp.bfloat16).reshape(2, N_FRAME, sub, 2 * block)
        dst = land.at[x, zb, pl.ds(pair * 2, 2)]
        local(ob.at[zb, :, f], dst, o_recv)

        @pl.loop(1, N_FRAME)
        def _(d):
            to = lax.rem(f + d, N_FRAME)
            remote(ob.at[zb, :, to], dst, o_send, o_recv, (c, to))

    def collect():
        wait(land, o_recv)
        pieces = [
            land[k, zb][:, :, yb * block : (yb + 1) * block].reshape(tok, block)
            for zb in range(n_z) for yb in range(2) for k in range(2)
        ]
        gh_ref[...] = jnp.concatenate(pieces, axis=1)

    steps = {
        "hidden": hidden, "spread": spread, "turn": turn, "plane": plane,
        "collect": collect,
    }
    for i in range(2):
        for h in range(n_z):
            steps["a" + str(i) + str(h)] = functools.partial(exchange, i, h)
        steps["swap" + str(i)] = functools.partial(swap, i)
        steps["attend" + str(i)] = functools.partial(attend, i)
        steps["share" + str(i)] = functools.partial(on_core, functools.partial(share, i))
    for name, fn in (
        ("own_y", w_start_y), ("own_z", w_start_z), ("y0", w_y0), ("ys", w_ys), ("weight", weight), ("sum_y", sum_y),
        ("sum_z", sum_z), ("finish", finish),
    ):
        steps[name] = functools.partial(on_core, fn)
    for i in range(1, n_z):
        steps["hop" + str(i)] = functools.partial(on_core, functools.partial(w_hop, i))
        steps["enter" + str(i)] = functools.partial(enter, i)
        steps["y" + str(i)] = functools.partial(on_core, functools.partial(w_ys, i))
    for j in range(n_z):
        steps["project" + str(j)] = functools.partial(project, j)
    for name in ORDER:
        steps[name]()

    for i in range(2):
        wait(leaving.at[:, pl.ds(0, N_FRAME - 1), :, slice(*PARTS[i])], a_send.at[i])
        wait(out_v.at[pl.ds(0, N_FRAME - 1), :, slice(*COLS[i])], b_send.at[i])
        wait(cat.at[0, :, :, slice(*COLS[i])], x_sem.at[0, i])
    wait(ob.at[:, :, pl.ds(0, N_FRAME - 1)], o_send)
    for i in range(3):
        wait(hs.at[0], h_send.at[i])


def per_device_fused(hidden, queries, keys, values, grad_attn, w_qkv):
    tok, width = hidden.shape[2], hidden.shape[3]
    inner = queries.shape[3]
    block, cat_w = w_qkv.shape
    flat = [
        jnp.swapaxes(a.reshape(tok, inner), 0, 1) for a in (queries, keys, values, grad_attn)
    ]
    bf, f32 = jnp.bfloat16, jnp.float32
    dma = pltpu.SemaphoreType.DMA
    sub, n_block, half = tok // N_FRAME, N_FRAME // 2, width // 2
    n_z = AX["z"][0]
    vmem = pltpu.VMEM
    scratch = (
        [vmem((inner, tok), bf)] * 4
        + [vmem((4, N_FRAME, sub, inner), bf)] * 2
        + [vmem((tok, width), bf), vmem((2, tok, half), bf), vmem((4, tok, half), bf)]
        + [vmem((n_block, block, high - low), bf) for low, high in W_COLS]
        + [vmem((tok, inner), f32)] * 3
        + [vmem((N_FRAME, sub, inner), bf), vmem((4, N_FRAME, sub, inner), bf)]
        + [vmem((2, 3, tok, inner), bf), vmem((2, tok, cat_w), bf)]
        + [vmem((n_z, 2, N_FRAME, sub, 2 * block), bf), vmem((2, n_z, N_FRAME, sub, 2 * block), bf)]
        + [vmem((n_block, block, inner), f32)]
        + [vmem((n_z, block, inner), bf)] * 4
        + [vmem((block, inner), f32)] * 2
        + [dma((3,)), dma((4,)), dma((2,)), dma((2,)), dma((2,)), dma((2,)), dma, dma((n_z, 2)), dma, dma((n_z, 2)), dma, dma((n_z,))]
        + [dma((3,)), dma((3,)), dma((2, 2)), dma((3,)), dma((3,)), dma, dma, dma((2,)), dma, dma, dma((2,))]
        + [pltpu.SemaphoreType.REGULAR, pltpu.SemaphoreType.REGULAR((n_z,))]
    )
    grad_hidden, grad_w = pl.pallas_call(
        kernel,
        out_shape=(
            pltpu.VMEM((tok, width), bf),
            pltpu.VMEM((block, inner), f32),
        ),
        in_specs=[pl.BlockSpec(memory_space=pl.ANY)] * 6,
        out_specs=(pl.BlockSpec(memory_space=pltpu.VMEM),) * 2,
        scratch_shapes=scratch,
        compiler_params=pltpu.CompilerParams(
            collective_id=0, has_side_effects=True, vmem_limit_bytes=60 * 1024 * 1024
        ),
    )(*flat, hidden.reshape(tok, width), w_qkv)
    return grad_hidden.reshape(hidden.shape), grad_w


def solution(mesh):
    in_specs = (
        P("clip", "frame", None, None),
        P("clip", "frame", None, None),
        P("clip", "frame", None, None),
        P("clip", "frame", None, None),
        P("clip", "frame", None, None),
        P("frame", None),
    )
    out_specs = (P("clip", "frame", None, None), P("frame", None))
    fused = mesh.shape["clip"] == 2 and mesh.shape["frame"] == N_FRAME
    return jax.shard_map(
        per_device_fused if fused else per_device, mesh=mesh, in_specs=in_specs, out_specs=out_specs, check_vma=False
    )
```

```python
import functools
import math

import jax
import jax.numpy as jnp
from jax import lax
from jax.experimental import pallas as pl
from jax.experimental.pallas import tpu as pltpu
from jax.sharding import PartitionSpec as P

HDIM = 104


def attend_back(queries, keys, values, grad_out):
    score_scale = 1.0 / math.sqrt(HDIM)
    scores = (
        jnp.einsum("fpnd,gpnd->pnfg", queries, keys, preferred_element_type=jnp.float32)
        * score_scale
    )
    attn_probs = jax.nn.softmax(scores, axis=-1)
    probs_bf = attn_probs.astype(jnp.bfloat16)
    grad_v = jnp.einsum(
        "pnfg,fpnd->gpnd", probs_bf, grad_out, preferred_element_type=jnp.float32
    ).astype(jnp.bfloat16)
    grad_probs = jnp.einsum("fpnd,gpnd->pnfg", grad_out, values, preferred_element_type=jnp.float32)
    grad_scores = attn_probs * (
        grad_probs - jnp.sum(attn_probs * grad_probs, axis=-1, keepdims=True)
    )
    scores_bf = grad_scores.astype(jnp.bfloat16)
    grad_q = (
        jnp.einsum("pnfg,gpnd->fpnd", scores_bf, keys, preferred_element_type=jnp.float32)
        * score_scale
    ).astype(jnp.bfloat16)
    grad_k = (
        jnp.einsum("pnfg,fpnd->gpnd", scores_bf, queries, preferred_element_type=jnp.float32)
        * score_scale
    ).astype(jnp.bfloat16)
    return (grad_q, grad_k, grad_v)


def per_device(hidden, queries, keys, values, grad_attn, w_qkv):
    frames_local = hidden.shape[1]
    patches = hidden.shape[2]
    model_width = hidden.shape[3]
    inner_width = queries.shape[3]
    head_count = inner_width // HDIM
    row_count = frames_local * patches
    head_shape = (frames_local, patches, head_count, HDIM)
    q_local = queries.reshape(head_shape)
    k_local = keys.reshape(head_shape)
    v_local = values.reshape(head_shape)
    g_local = grad_attn.reshape(head_shape)
    q_patch, k_patch, v_patch, g_patch = (
        lax.all_to_all(q_local, "frame", split_axis=1, concat_axis=0, tiled=True),
        lax.all_to_all(k_local, "frame", split_axis=1, concat_axis=0, tiled=True),
        lax.all_to_all(v_local, "frame", split_axis=1, concat_axis=0, tiled=True),
        lax.all_to_all(g_local, "frame", split_axis=1, concat_axis=0, tiled=True),
    )
    grad_q, grad_k, grad_v = attend_back(q_patch, k_patch, v_patch, g_patch)
    grad_q, grad_k, grad_v = (
        lax.all_to_all(grad_q, "frame", split_axis=0, concat_axis=1, tiled=True),
        lax.all_to_all(grad_k, "frame", split_axis=0, concat_axis=1, tiled=True),
        lax.all_to_all(grad_v, "frame", split_axis=0, concat_axis=1, tiled=True),
    )
    value_rows = grad_v.reshape(row_count, inner_width)
    grad_cat = jnp.concatenate(
        [
            grad_q.reshape(row_count, inner_width),
            grad_k.reshape(row_count, inner_width),
            value_rows,
        ],
        axis=1,
    )
    grad_hid = lax.dot_general(
        grad_cat,
        lax.all_gather(w_qkv, "frame", axis=0, tiled=True),
        (((1,), (1,)), ((), ())),
        preferred_element_type=jnp.float32,
    )
    grad_hidden = grad_hid.astype(jnp.bfloat16).reshape(hidden.shape)
    hidden_rows = hidden.reshape(row_count, model_width)
    clip_count = lax.axis_size("clip")
    partial_grad = lax.psum_scatter(
        lax.dot_general(
            hidden_rows, value_rows, (((0,), (0,)), ((), ())), preferred_element_type=jnp.float32
        ),
        "frame",
        scatter_dimension=0,
        tiled=True,
    )
    grad_total = lax.psum(partial_grad, "clip")
    return (grad_hidden, grad_total / clip_count)


AX = {"z": (4, 4), "y": (2, 2), "x": (2, 1)}
N_FRAME = 16
ORDER = (
    "own_y", "own_z", "turn", "plane", "a00", "enter1", "a01", "enter2", "a02", "enter3", "a03",
    "a10", "a11", "a12", "a13", "hop1", "hidden", "spread", "y0", "attend0", "swap0", "attend1", "swap1",
    "hop2", "share0", "share1", "hop3", "y1", "y2", "y3", "weight_here", "weight", "project0", "project1", "project2",
    "project3", "sum_y", "collect", "sum_z", "finish",
)
NEAR = (1, 2, 0, 3)
COLS = ((0, 384), (384, 832))
PARTS = ((0, 512), (512, 832))
W_COLS = ((0, 1280), (1280, 2496))
W_CUT = 640


def move(f, axis, k):
    size, stride = AX[axis]
    digit = lax.rem(lax.div(f, stride), size)
    return f + (lax.rem(digit + k, size) - digit) * stride


def kernel(
    q_hbm, k_hbm, v_hbm, g_hbm, h_hbm, w_hbm,
    gh_ref, gw_ref,
    tq, tk, tv, tg, leaving, arrived,
    hb, hs, hall, w0, w1, acc_q, acc_k, acc_v, out_v, gall, cat, joined, ob, land,
    dws, y_s, y_r, z_s, z_r, fin_s, fin_r,
    loc, t_sem, a_send, a_recv, b_send, b_recv, wy_send, wy_recv, wz_send, wz_recv, wc_send, wc_recv,
    h_send, h_recv, x_sem, g_send, g_recv, o_send, o_recv, ry_sem, rz_send, rz_recv, f_sem, plane_sem, in_sem,
):
    c = lax.axis_index("clip")
    f = lax.axis_index("frame")
    other = 1 - c
    block = w_hbm.shape[0]
    tok = q_hbm.shape[1]
    sub = tok // N_FRAME
    n_block = w0.shape[0]
    n_z = AX["z"][0]
    last = n_z - 1
    scale = 1.0 / math.sqrt(HDIM)
    x = lax.rem(f, 2)
    pair = lax.div(f, 2)
    y = lax.rem(pair, 2)
    z = lax.div(pair, 2)
    beside = f + 1 - 2 * x
    across = move(f, "y", 1)
    slot = x * 2 + c

    def remote(src, dst, ss, rs, peer):
        pltpu.make_async_remote_copy(
            src_ref=src, dst_ref=dst, send_sem=ss, recv_sem=rs,
            device_id=peer, device_id_type=pl.DeviceIdType.MESH,
        ).start()

    def local(src, dst, sem):
        pltpu.make_async_copy(src, dst, sem).start()

    def wait(view, sem):
        pltpu.make_async_copy(view, view, sem).wait()

    def on_core(fn):
        for core in range(2):
            pl.when(c == core)(functools.partial(fn, core))

    barrier = pltpu.get_barrier_semaphore()

    def greet(peer):
        pl.semaphore_signal(barrier, inc=1, device_id=peer, device_id_type=pl.DeviceIdType.MESH)

    for peer in ((c, beside), (c, across), (other, f), (other, beside)):
        greet(peer)
    for way in (1, -1):

        @pl.when((z < last) if way == 1 else (z > 0))
        def _():
            greet((c, f + way * AX["z"][1]))

    turned = ((q_hbm, tq), (k_hbm, tk), (g_hbm, tg), (v_hbm, tv))
    pairs = [(leaving.at[i], arrived.at[i]) for i in range(4)]
    qb, kb, gb, vb = (arrived.at[i] for i in range(4))
    for i, (src, flat) in enumerate(turned):
        local(src, flat, t_sem.at[i])
    local(h_hbm, hb, loc.at[0])
    w_part = (w0, w1)
    for i in range(2):
        local(w_hbm.at[:, slice(*W_COLS[i])], w_part[i].at[pair], loc.at[1 + i])
    pl.semaphore_wait(barrier, 6 - jnp.where((z == 0) | (z == last), 1, 0))

    def tell(sem, peer):
        pl.semaphore_signal(sem, inc=1, device_id=peer, device_id_type=pl.DeviceIdType.MESH)

    def pass_in(from_z, way):
        @pl.when((z < last) if way == 1 else (z > 0))
        def _():
            tell(in_sem.at[from_z], (c, f + way * AX["z"][1]))

    def plane():
        tell(plane_sem, (c, across))
        pl.semaphore_wait(plane_sem, 1)
        for way in (1, -1):
            pass_in(z, way)

    def enter(h):
        for way in (1, -1):
            from_z = z - way * h

            @pl.when((from_z >= 0) & (from_z <= last))
            def _():
                pl.semaphore_wait(in_sem.at[from_z], 1)
                pass_in(from_z, way)

    def cut(core, k):
        return slice(0, W_CUT) if k == 0 else slice(W_CUT, w_part[core].shape[2])

    def w_at(core, zb, yb, k):
        return w_part[core].at[zb * 2 + yb, :, cut(core, k)]

    def w_wait(core, k, sem):
        wait(w_part[core].at[0, :, cut(core, k)], sem)

    def forward(core, zb, yb, k):
        view = w_at(core, zb, yb, k)
        remote(view, view, wc_send, wc_recv.at[zb], (other, f))

    def pass_y(core, zb, k, src=None):
        dst = w_at(core, zb, y, k)
        remote(dst if src is None else src, dst, wy_send, wy_recv.at[zb, k], (c, across))

    def climb(core, zb, way, k, src=None):
        dst = w_at(core, zb, y, k)

        @pl.when((z < last) if way == 1 else (z > 0))
        def _():
            peer = (c, f + way * AX["z"][1])
            remote(dst if src is None else src, dst, wz_send, wz_recv.at[zb, k], peer)

    def own(core, k):
        low, high = W_COLS[core]
        return w_hbm.at[:, (slice(low, low + W_CUT) if k == 0 else slice(low + W_CUT, high))]

    def w_start_y(core):
        for k in range(2):
            pass_y(core, z, k, own(core, k))

    def w_start_z(core):
        for k in range(2):
            for way in (1, -1):
                climb(core, z, way, k, own(core, k))

    def w_hop(h, core):
        for k in range(2):
            for way in (1, -1):
                from_z = z - way * h

                @pl.when((from_z >= 0) & (from_z <= last))
                def _():
                    w_wait(core, k, wz_recv.at[from_z, k])
                    climb(core, from_z, way, k)
                    pass_y(core, from_z, k)
                    forward(core, from_z, y, k)

    def w_y0(core):
        for k in range(2):
            w_wait(core, k, wy_recv.at[z, k])
            forward(core, z, 1 - y, k)

    def by_distance(j):
        at_end = (z == 0) | (z == last)
        up = jnp.where(at_end, j, NEAR[j])
        return jnp.where(z * 2 < n_z, up, last - up)

    def w_ys(j, core):
        zb = by_distance(j)
        for k in range(2):
            w_wait(core, k, wy_recv.at[zb, k])
            forward(core, zb, 1 - y, k)

    def w_drain(core):
        wait(w_part[core].at[pl.ds(0, n_z)], wy_send)
        edge = (z == 0) | (z == last)
        for ends, count in ((True, 1), (False, 5)):

            @pl.when(edge if ends else jnp.logical_not(edge))
            def _():
                wait(w_part[core].at[pl.ds(0, count)], wz_send)

        wait(w_part[core].at[pl.ds(0, n_block - 1)], wc_send)

    def turn():
        for i, (src, _) in enumerate(pairs):
            pltpu.make_async_copy(turned[i][0], turned[i][1], t_sem.at[i]).wait()
            src[...] = turned[i][1][...].T.reshape(src.shape)

    def exchange(part, h):
        cols = slice(*PARTS[part])

        def to_frame(to):
            for src, dst in pairs:
                remote(src.at[to, :, cols], dst.at[f, :, cols], a_send.at[part], a_recv.at[part], (c, to))

        if h == 0:
            for src, dst in pairs:
                local(src.at[f, :, cols], dst.at[f, :, cols], a_recv.at[part])
            for to in (beside, across, move(across, "x", 1)):
                to_frame(to)
            return
        for way in (1, -1):
            to_z = z - way * h

            @pl.when((to_z >= 0) & (to_z <= last))
            def _():
                @pl.loop(0, AX["z"][1])
                def _(k):
                    to_frame(to_z * AX["z"][1] + k)

    acc_q[...] = jnp.zeros_like(acc_q)
    acc_k[...] = jnp.zeros_like(acc_k)
    acc_v[...] = jnp.zeros_like(acc_v)
    row_id = lax.broadcasted_iota(jnp.int32, (tok, tok), 0)
    col_id = lax.broadcasted_iota(jnp.int32, (tok, tok), 1)
    same = lax.rem(row_id, sub) == lax.rem(col_id, sub)

    width_all = q_hbm.shape[0]
    heads = width_all // HDIM
    nt = (((1,), (1,)), ((), ()))
    tn = (((0,), (0,)), ((), ()))
    nn = (((1,), (0,)), ((), ()))
    dot = functools.partial(lax.dot_general, preferred_element_type=jnp.float32)

    def window(n):
        low = n * HDIM // 128 * 128
        high = min(-(-(n + 1) * HDIM // 128) * 128, width_all)
        lane = lax.broadcasted_iota(jnp.int32, (tok, high - low), 1) + low
        keep = jnp.where((lane >= n * HDIM) & (lane < (n + 1) * HDIM), 1.0, 0.0)
        return slice(low, high), keep.astype(jnp.bfloat16)

    def rows(ref, win):
        return ref[:, :, win].reshape(tok, win.stop - win.start)

    def hidden():
        pltpu.make_async_copy(h_hbm, hb, loc.at[0]).wait()
        for k in range(2):
            half = jnp.concatenate(
                [hb[:, (2 * i + k) * block : (2 * i + k + 1) * block] for i in range(n_block)], axis=1
            )
            hs[k] = half
        hall[slot] = hs[x]
        remote(hs.at[1 - x], hall.at[slot], h_send.at[0], h_recv.at[0], (c, beside))
        remote(hs.at[x], hall.at[slot], h_send.at[1], h_recv.at[1], (other, f))

    def spread():
        theirs = hall.at[(1 - x) * 2 + c]
        wait(theirs, h_recv.at[0])
        remote(theirs, theirs, h_send.at[2], h_recv.at[2], (other, f))

    def attend(part):
        wait(arrived.at[:, :, :, slice(*PARTS[part])], a_recv.at[part])
        half = heads // 2
        for n in range(part * half, (part + 1) * half):
            win, keep = window(n)
            g = rows(gb, win) * keep
            s = dot(rows(qb, win) * keep, rows(kb, win), nt) * scale
            s = jnp.where(same, s, -1e30)
            e = jnp.exp(s - jnp.max(s, axis=1, keepdims=True))
            p = e / jnp.sum(e, axis=1, keepdims=True)
            acc_v[:, win] += dot(p.astype(jnp.bfloat16), g, tn)
            dp = dot(g, rows(vb, win), nt)
            ds = (p * (dp - jnp.sum(p * dp, axis=1, keepdims=True))).astype(jnp.bfloat16)
            acc_q[:, win] += dot(ds, rows(kb, win) * keep, nn)
            acc_k[:, win] += dot(ds, rows(qb, win) * keep, tn)
        cols = slice(*COLS[part])
        grad_v = acc_v[:, cols].astype(jnp.bfloat16)
        out_v[:, :, cols] = grad_v.reshape(N_FRAME, sub, cols.stop - cols.start)
        local(out_v.at[f, :, cols], gall.at[slot, f, :, cols], b_recv.at[part])

        @pl.loop(1, N_FRAME)
        def _(d):
            to = lax.rem(f + d, N_FRAME)
            dst = gall.at[lax.rem(to, 2) * 2 + c, f, :, cols]
            remote(out_v.at[to, :, cols], dst, b_send.at[part], b_recv.at[part], (c, to))

        cat[x, 0, :, cols] = (acc_q[:, cols] * scale).astype(jnp.bfloat16)
        cat[x, 1, :, cols] = (acc_k[:, cols] * scale).astype(jnp.bfloat16)
        cat[x, 2, :, cols] = grad_v

    def swap(part):
        mine = cat.at[x, :, :, slice(*COLS[part])]
        remote(mine, mine, x_sem.at[0, part], x_sem.at[1, part], (c, beside))

    def share(to, core):
        wait(gall.at[0, :, :, slice(*COLS[to])], b_recv.at[to])
        src = gall.at[slot, :, :, slice(*COLS[to])]
        remote(src, src, g_send.at[to], g_recv.at[0 if to == core else 1], (to, beside))
        if to != core:
            remote(src, src, g_send.at[2], g_recv.at[2], (to, f))

    def token_sum(side, cols):
        n = cols.stop - cols.start
        both = pl.ds(side * 2, 2)
        total = dot(
            hall[both].reshape(2 * tok, hall.shape[2]), gall[both, :, :, cols].reshape(2 * tok, n), tn
        )
        return total.reshape(n_block, block, n)

    def weight_here(core):
        cols = slice(*COLS[core])
        wait(hall.at[0], h_recv.at[1])
        wait(gall.at[0, :, :, cols], g_recv.at[2])
        dws[:, :, cols] = token_sum(x, cols)

    def weight(core):
        cols = slice(*COLS[core])
        wait(hall.at[0], h_recv.at[2])
        for i in range(2):
            wait(gall.at[0, :, :, cols], g_recv.at[i])
        dws[:, :, cols] += token_sum(1 - x, cols)
        for zb in range(n_z):
            y_s[zb, :, cols] = dws[zb * 2 + 1 - y, :, cols].astype(jnp.bfloat16)
        remote(y_s.at[:, :, cols], y_r.at[:, :, cols], ry_sem.at[0], ry_sem.at[1], (c, across))

    def sum_y(core):
        cols = slice(*COLS[core])
        wait(y_r.at[:, :, cols], ry_sem.at[1])
        for k in range(1, n_z):
            zb = lax.rem(z + k, n_z)
            total = dws[zb * 2 + y, :, cols] + y_r[zb, :, cols].astype(jnp.float32)
            z_s[zb, :, cols] = total.astype(jnp.bfloat16)
            remote(z_s.at[zb, :, cols], z_r.at[z, :, cols], rz_send, rz_recv, (c, move(f, "z", k)))
        dws[pair, :, cols] += y_r[z, :, cols].astype(jnp.float32)

    def sum_z(core):
        cols = slice(*COLS[core])
        wait(z_r.at[pl.ds(0, n_z - 1), :, cols], rz_recv)
        total = dws[pair, :, cols]
        for k in range(1, n_z):
            total += z_r[lax.rem(z + k, n_z), :, cols].astype(jnp.float32)
        total *= 0.5
        fin_s[:, cols] = total
        remote(fin_s.at[:, cols], fin_r.at[:, cols], f_sem.at[0], f_sem.at[1], (other, f))
        gw_ref[:, cols] = total

    def finish(core):
        mine, rest = slice(*COLS[core]), slice(*COLS[1 - core])
        wait(fin_r.at[:, rest], f_sem.at[1])
        gw_ref[:, rest] = fin_r[:, rest]
        wait(fin_s.at[:, mine], f_sem.at[0])
        wait(y_s.at[:, :, mine], ry_sem.at[0])
        wait(z_s.at[pl.ds(0, n_z - 1), :, mine], rz_send)
        for to in range(2):
            wait(gall.at[0, :, :, slice(*COLS[to])], g_send.at[to])
            if to != core:
                wait(gall.at[0, :, :, slice(*COLS[to])], g_send.at[2])
        w_drain(core)

    def project(j):
        zb = by_distance(j)
        if j == 0:
            for i in range(2):
                wait(cat.at[0, :, :, slice(*COLS[i])], x_sem.at[1, i])
                pltpu.make_async_copy(w_hbm.at[:, slice(*W_COLS[i])], w_part[i].at[pair], loc.at[1 + i]).wait()
        on_core(lambda core: wait(w_part[1 - core].at[pl.ds(0, 2 if j else 1)], wc_recv.at[zb]))
        if j == 0:
            for k in range(2):
                joined[k] = jnp.concatenate([cat[k, i] for i in range(3)], axis=1)
        grads = joined[...].reshape(2 * tok, joined.shape[2])
        parts = [w[pl.ds(zb * 2, 2)].reshape(2 * block, w.shape[2]) for w in w_part]
        res = sum(dot(grads[:, slice(*W_COLS[i])], parts[i], nt) for i in range(2))
        ob[zb] = res.astype(jnp.bfloat16).reshape(2, N_FRAME, sub, 2 * block)
        dst = land.at[x, zb, pl.ds(pair * 2, 2)]
        local(ob.at[zb, :, f], dst, o_recv)

        @pl.loop(1, N_FRAME)
        def _(d):
            to = lax.rem(f + d, N_FRAME)
            remote(ob.at[zb, :, to], dst, o_send, o_recv, (c, to))

    def collect():
        wait(land, o_recv)
        pieces = [
            land[k, zb][:, :, yb * block : (yb + 1) * block].reshape(tok, block)
            for zb in range(n_z) for yb in range(2) for k in range(2)
        ]
        gh_ref[...] = jnp.concatenate(pieces, axis=1)

    steps = {
        "hidden": hidden, "spread": spread, "turn": turn, "plane": plane,
        "collect": collect,
    }
    for i in range(2):
        for h in range(n_z):
            steps["a" + str(i) + str(h)] = functools.partial(exchange, i, h)
        steps["swap" + str(i)] = functools.partial(swap, i)
        steps["attend" + str(i)] = functools.partial(attend, i)
        steps["share" + str(i)] = functools.partial(on_core, functools.partial(share, i))
    for name, fn in (
        ("own_y", w_start_y), ("own_z", w_start_z), ("y0", w_y0), ("ys", w_ys), ("weight", weight), ("weight_here", weight_here), ("sum_y", sum_y),
        ("sum_z", sum_z), ("finish", finish),
    ):
        steps[name] = functools.partial(on_core, fn)
    for i in range(1, n_z):
        steps["hop" + str(i)] = functools.partial(on_core, functools.partial(w_hop, i))
        steps["enter" + str(i)] = functools.partial(enter, i)
        steps["y" + str(i)] = functools.partial(on_core, functools.partial(w_ys, i))
    for j in range(n_z):
        steps["project" + str(j)] = functools.partial(project, j)
    for name in ORDER:
        steps[name]()

    for i in range(2):
        wait(leaving.at[:, pl.ds(0, N_FRAME - 1), :, slice(*PARTS[i])], a_send.at[i])
        wait(out_v.at[pl.ds(0, N_FRAME - 1), :, slice(*COLS[i])], b_send.at[i])
        wait(cat.at[0, :, :, slice(*COLS[i])], x_sem.at[0, i])
    wait(ob.at[:, :, pl.ds(0, N_FRAME - 1)], o_send)
    for i in range(3):
        wait(hs.at[0], h_send.at[i])


def per_device_fused(hidden, queries, keys, values, grad_attn, w_qkv):
    tok, width = hidden.shape[2], hidden.shape[3]
    inner = queries.shape[3]
    block, cat_w = w_qkv.shape
    flat = [
        jnp.swapaxes(a.reshape(tok, inner), 0, 1) for a in (queries, keys, values, grad_attn)
    ]
    bf, f32 = jnp.bfloat16, jnp.float32
    dma = pltpu.SemaphoreType.DMA
    sub, n_block, half = tok // N_FRAME, N_FRAME // 2, width // 2
    n_z = AX["z"][0]
    vmem = pltpu.VMEM
    scratch = (
        [vmem((inner, tok), bf)] * 4
        + [vmem((4, N_FRAME, sub, inner), bf)] * 2
        + [vmem((tok, width), bf), vmem((2, tok, half), bf), vmem((4, tok, half), bf)]
        + [vmem((n_block, block, high - low), bf) for low, high in W_COLS]
        + [vmem((tok, inner), f32)] * 3
        + [vmem((N_FRAME, sub, inner), bf), vmem((4, N_FRAME, sub, inner), bf)]
        + [vmem((2, 3, tok, inner), bf), vmem((2, tok, cat_w), bf)]
        + [vmem((n_z, 2, N_FRAME, sub, 2 * block), bf), vmem((2, n_z, N_FRAME, sub, 2 * block), bf)]
        + [vmem((n_block, block, inner), f32)]
        + [vmem((n_z, block, inner), bf)] * 4
        + [vmem((block, inner), f32)] * 2
        + [dma((3,)), dma((4,)), dma((2,)), dma((2,)), dma((2,)), dma((2,)), dma, dma((n_z, 2)), dma, dma((n_z, 2)), dma, dma((n_z,))]
        + [dma((3,)), dma((3,)), dma((2, 2)), dma((3,)), dma((3,)), dma, dma, dma((2,)), dma, dma, dma((2,))]
        + [pltpu.SemaphoreType.REGULAR, pltpu.SemaphoreType.REGULAR((n_z,))]
    )
    grad_hidden, grad_w = pl.pallas_call(
        kernel,
        out_shape=(
            pltpu.VMEM((tok, width), bf),
            pltpu.VMEM((block, inner), f32),
        ),
        in_specs=[pl.BlockSpec(memory_space=pl.ANY)] * 6,
        out_specs=(pl.BlockSpec(memory_space=pltpu.VMEM),) * 2,
        scratch_shapes=scratch,
        compiler_params=pltpu.CompilerParams(
            collective_id=0, has_side_effects=True, vmem_limit_bytes=60 * 1024 * 1024
        ),
    )(*flat, hidden.reshape(tok, width), w_qkv)
    return grad_hidden.reshape(hidden.shape), grad_w


def solution(mesh):
    in_specs = (
        P("clip", "frame", None, None),
        P("clip", "frame", None, None),
        P("clip", "frame", None, None),
        P("clip", "frame", None, None),
        P("clip", "frame", None, None),
        P("frame", None),
    )
    out_specs = (P("clip", "frame", None, None), P("frame", None))
    fused = mesh.shape["clip"] == 2 and mesh.shape["frame"] == N_FRAME
    return jax.shard_map(
        per_device_fused if fused else per_device, mesh=mesh, in_specs=in_specs, out_specs=out_specs, check_vma=False
    )
```

```python
import functools
import math

import jax
import jax.numpy as jnp
from jax import lax
from jax.experimental import pallas as pl
from jax.experimental.pallas import tpu as pltpu
from jax.sharding import PartitionSpec as P

HDIM = 104


def attend_back(queries, keys, values, grad_out):
    score_scale = 1.0 / math.sqrt(HDIM)
    scores = (
        jnp.einsum("fpnd,gpnd->pnfg", queries, keys, preferred_element_type=jnp.float32)
        * score_scale
    )
    attn_probs = jax.nn.softmax(scores, axis=-1)
    probs_bf = attn_probs.astype(jnp.bfloat16)
    grad_v = jnp.einsum(
        "pnfg,fpnd->gpnd", probs_bf, grad_out, preferred_element_type=jnp.float32
    ).astype(jnp.bfloat16)
    grad_probs = jnp.einsum("fpnd,gpnd->pnfg", grad_out, values, preferred_element_type=jnp.float32)
    grad_scores = attn_probs * (
        grad_probs - jnp.sum(attn_probs * grad_probs, axis=-1, keepdims=True)
    )
    scores_bf = grad_scores.astype(jnp.bfloat16)
    grad_q = (
        jnp.einsum("pnfg,gpnd->fpnd", scores_bf, keys, preferred_element_type=jnp.float32)
        * score_scale
    ).astype(jnp.bfloat16)
    grad_k = (
        jnp.einsum("pnfg,fpnd->gpnd", scores_bf, queries, preferred_element_type=jnp.float32)
        * score_scale
    ).astype(jnp.bfloat16)
    return (grad_q, grad_k, grad_v)


def per_device(hidden, queries, keys, values, grad_attn, w_qkv):
    frames_local = hidden.shape[1]
    patches = hidden.shape[2]
    model_width = hidden.shape[3]
    inner_width = queries.shape[3]
    head_count = inner_width // HDIM
    row_count = frames_local * patches
    head_shape = (frames_local, patches, head_count, HDIM)
    q_local = queries.reshape(head_shape)
    k_local = keys.reshape(head_shape)
    v_local = values.reshape(head_shape)
    g_local = grad_attn.reshape(head_shape)
    q_patch, k_patch, v_patch, g_patch = (
        lax.all_to_all(q_local, "frame", split_axis=1, concat_axis=0, tiled=True),
        lax.all_to_all(k_local, "frame", split_axis=1, concat_axis=0, tiled=True),
        lax.all_to_all(v_local, "frame", split_axis=1, concat_axis=0, tiled=True),
        lax.all_to_all(g_local, "frame", split_axis=1, concat_axis=0, tiled=True),
    )
    grad_q, grad_k, grad_v = attend_back(q_patch, k_patch, v_patch, g_patch)
    grad_q, grad_k, grad_v = (
        lax.all_to_all(grad_q, "frame", split_axis=0, concat_axis=1, tiled=True),
        lax.all_to_all(grad_k, "frame", split_axis=0, concat_axis=1, tiled=True),
        lax.all_to_all(grad_v, "frame", split_axis=0, concat_axis=1, tiled=True),
    )
    value_rows = grad_v.reshape(row_count, inner_width)
    grad_cat = jnp.concatenate(
        [
            grad_q.reshape(row_count, inner_width),
            grad_k.reshape(row_count, inner_width),
            value_rows,
        ],
        axis=1,
    )
    grad_hid = lax.dot_general(
        grad_cat,
        lax.all_gather(w_qkv, "frame", axis=0, tiled=True),
        (((1,), (1,)), ((), ())),
        preferred_element_type=jnp.float32,
    )
    grad_hidden = grad_hid.astype(jnp.bfloat16).reshape(hidden.shape)
    hidden_rows = hidden.reshape(row_count, model_width)
    clip_count = lax.axis_size("clip")
    partial_grad = lax.psum_scatter(
        lax.dot_general(
            hidden_rows, value_rows, (((0,), (0,)), ((), ())), preferred_element_type=jnp.float32
        ),
        "frame",
        scatter_dimension=0,
        tiled=True,
    )
    grad_total = lax.psum(partial_grad, "clip")
    return (grad_hidden, grad_total / clip_count)


AX = {"z": (4, 4), "y": (2, 2), "x": (2, 1)}
N_FRAME = 16
ORDER = (
    "own_y", "own_z", "turn", "plane", "a00", "enter1", "a01", "enter2", "a02", "enter3", "a03",
    "a10", "a11", "a12", "a13", "hop1", "hidden", "spread", "y0", "attend0", "swap0", "attend1", "swap1",
    "hop2", "share0", "share1", "hop3", "y1", "y2", "y3", "weight_here", "weight", "project0", "project1", "project2",
    "project3", "sum_y", "collect", "sum_z", "finish",
)
NEAR = (1, 2, 0, 3)
COLS = ((0, 384), (384, 832))
PARTS = ((0, 512), (512, 832))
W_COLS = ((0, 1152), (1152, 2496))
W_CUT = 512


def move(f, axis, k):
    size, stride = AX[axis]
    digit = lax.rem(lax.div(f, stride), size)
    return f + (lax.rem(digit + k, size) - digit) * stride


def kernel(
    q_hbm, k_hbm, v_hbm, g_hbm, h_hbm, w_hbm,
    gh_ref, gw_ref,
    tq, tk, tv, tg, leaving, arrived,
    hb, hs, hall, w0, w1, acc_q, acc_k, acc_v, out_v, gall, cat, joined, ob, land,
    dws, y_s, y_r, z_s, z_r, fin_s, fin_r,
    loc, t_sem, a_send, a_recv, b_send, b_recv, wy_send, wy_recv, wz_send, wz_recv, wc_send, wc_recv,
    h_send, h_recv, x_sem, g_send, g_recv, o_send, o_recv, ry_sem, rz_send, rz_recv, f_sem, plane_sem, in_sem,
):
    c = lax.axis_index("clip")
    f = lax.axis_index("frame")
    other = 1 - c
    block = w_hbm.shape[0]
    tok = q_hbm.shape[1]
    sub = tok // N_FRAME
    n_block = w0.shape[0]
    n_z = AX["z"][0]
    last = n_z - 1
    scale = 1.0 / math.sqrt(HDIM)
    x = lax.rem(f, 2)
    pair = lax.div(f, 2)
    y = lax.rem(pair, 2)
    z = lax.div(pair, 2)
    beside = f + 1 - 2 * x
    across = move(f, "y", 1)
    slot = x * 2 + c

    def remote(src, dst, ss, rs, peer):
        pltpu.make_async_remote_copy(
            src_ref=src, dst_ref=dst, send_sem=ss, recv_sem=rs,
            device_id=peer, device_id_type=pl.DeviceIdType.MESH,
        ).start()

    def local(src, dst, sem):
        pltpu.make_async_copy(src, dst, sem).start()

    def wait(view, sem):
        pltpu.make_async_copy(view, view, sem).wait()

    def on_core(fn):
        for core in range(2):
            pl.when(c == core)(functools.partial(fn, core))

    barrier = pltpu.get_barrier_semaphore()

    def greet(peer):
        pl.semaphore_signal(barrier, inc=1, device_id=peer, device_id_type=pl.DeviceIdType.MESH)

    for peer in ((c, beside), (c, across), (other, f), (other, beside)):
        greet(peer)
    for way in (1, -1):

        @pl.when((z < last) if way == 1 else (z > 0))
        def _():
            greet((c, f + way * AX["z"][1]))

    turned = ((q_hbm, tq), (k_hbm, tk), (g_hbm, tg), (v_hbm, tv))
    pairs = [(leaving.at[i], arrived.at[i]) for i in range(4)]
    qb, kb, gb, vb = (arrived.at[i] for i in range(4))
    for i, (src, flat) in enumerate(turned):
        local(src, flat, t_sem.at[i])
    local(h_hbm, hb, loc.at[0])
    w_part = (w0, w1)
    for i in range(2):
        local(w_hbm.at[:, slice(*W_COLS[i])], w_part[i].at[pair], loc.at[1 + i])
    pl.semaphore_wait(barrier, 6 - jnp.where((z == 0) | (z == last), 1, 0))

    def tell(sem, peer):
        pl.semaphore_signal(sem, inc=1, device_id=peer, device_id_type=pl.DeviceIdType.MESH)

    def pass_in(from_z, way):
        @pl.when((z < last) if way == 1 else (z > 0))
        def _():
            tell(in_sem.at[from_z], (c, f + way * AX["z"][1]))

    def plane():
        tell(plane_sem, (c, across))
        pl.semaphore_wait(plane_sem, 1)
        for way in (1, -1):
            pass_in(z, way)

    def enter(h):
        for way in (1, -1):
            from_z = z - way * h

            @pl.when((from_z >= 0) & (from_z <= last))
            def _():
                pl.semaphore_wait(in_sem.at[from_z], 1)
                pass_in(from_z, way)

    def cut(core, k):
        return slice(0, W_CUT) if k == 0 else slice(W_CUT, w_part[core].shape[2])

    def w_at(core, zb, yb, k):
        return w_part[core].at[zb * 2 + yb, :, cut(core, k)]

    def w_wait(core, k, sem):
        wait(w_part[core].at[0, :, cut(core, k)], sem)

    def forward(core, zb, yb, k):
        view = w_at(core, zb, yb, k)
        remote(view, view, wc_send, wc_recv.at[zb], (other, f))

    def pass_y(core, zb, k, src=None):
        dst = w_at(core, zb, y, k)
        remote(dst if src is None else src, dst, wy_send, wy_recv.at[zb, k], (c, across))

    def climb(core, zb, way, k, src=None):
        dst = w_at(core, zb, y, k)

        @pl.when((z < last) if way == 1 else (z > 0))
        def _():
            peer = (c, f + way * AX["z"][1])
            remote(dst if src is None else src, dst, wz_send, wz_recv.at[zb, k], peer)

    def own(core, k):
        low, high = W_COLS[core]
        return w_hbm.at[:, (slice(low, low + W_CUT) if k == 0 else slice(low + W_CUT, high))]

    def w_start_y(core):
        for k in range(2):
            pass_y(core, z, k, own(core, k))

    def w_start_z(core):
        for k in range(2):
            for way in (1, -1):
                climb(core, z, way, k, own(core, k))

    def w_hop(h, core):
        for k in range(2):
            for way in (1, -1):
                from_z = z - way * h

                @pl.when((from_z >= 0) & (from_z <= last))
                def _():
                    w_wait(core, k, wz_recv.at[from_z, k])
                    climb(core, from_z, way, k)
                    pass_y(core, from_z, k)
                    forward(core, from_z, y, k)

    def w_y0(core):
        for k in range(2):
            w_wait(core, k, wy_recv.at[z, k])
            forward(core, z, 1 - y, k)

    def by_distance(j):
        at_end = (z == 0) | (z == last)
        up = jnp.where(at_end, j, NEAR[j])
        return jnp.where(z * 2 < n_z, up, last - up)

    def w_ys(j, core):
        zb = by_distance(j)
        for k in range(2):
            w_wait(core, k, wy_recv.at[zb, k])
            forward(core, zb, 1 - y, k)

    def w_drain(core):
        wait(w_part[core].at[pl.ds(0, n_z)], wy_send)
        edge = (z == 0) | (z == last)
        for ends, count in ((True, 1), (False, 5)):

            @pl.when(edge if ends else jnp.logical_not(edge))
            def _():
                wait(w_part[core].at[pl.ds(0, count)], wz_send)

        wait(w_part[core].at[pl.ds(0, n_block - 1)], wc_send)

    def turn():
        for i, (src, _) in enumerate(pairs):
            pltpu.make_async_copy(turned[i][0], turned[i][1], t_sem.at[i]).wait()
            src[...] = turned[i][1][...].T.reshape(src.shape)

    def exchange(part, h):
        cols = slice(*PARTS[part])

        def to_frame(to):
            for src, dst in pairs:
                remote(src.at[to, :, cols], dst.at[f, :, cols], a_send.at[part], a_recv.at[part], (c, to))

        if h == 0:
            for src, dst in pairs:
                local(src.at[f, :, cols], dst.at[f, :, cols], a_recv.at[part])
            for to in (beside, across, move(across, "x", 1)):
                to_frame(to)
            return
        for way in (1, -1):
            to_z = z - way * h

            @pl.when((to_z >= 0) & (to_z <= last))
            def _():
                @pl.loop(0, AX["z"][1])
                def _(k):
                    to_frame(to_z * AX["z"][1] + k)

    acc_q[...] = jnp.zeros_like(acc_q)
    acc_k[...] = jnp.zeros_like(acc_k)
    acc_v[...] = jnp.zeros_like(acc_v)
    row_id = lax.broadcasted_iota(jnp.int32, (tok, tok), 0)
    col_id = lax.broadcasted_iota(jnp.int32, (tok, tok), 1)
    same = lax.rem(row_id, sub) == lax.rem(col_id, sub)

    width_all = q_hbm.shape[0]
    heads = width_all // HDIM
    nt = (((1,), (1,)), ((), ()))
    tn = (((0,), (0,)), ((), ()))
    nn = (((1,), (0,)), ((), ()))
    dot = functools.partial(lax.dot_general, preferred_element_type=jnp.float32)

    def window(n):
        low = n * HDIM // 128 * 128
        high = min(-(-(n + 1) * HDIM // 128) * 128, width_all)
        lane = lax.broadcasted_iota(jnp.int32, (tok, high - low), 1) + low
        keep = jnp.where((lane >= n * HDIM) & (lane < (n + 1) * HDIM), 1.0, 0.0)
        return slice(low, high), keep.astype(jnp.bfloat16)

    def rows(ref, win):
        return ref[:, :, win].reshape(tok, win.stop - win.start)

    def hidden():
        pltpu.make_async_copy(h_hbm, hb, loc.at[0]).wait()
        for k in range(2):
            half = jnp.concatenate(
                [hb[:, (2 * i + k) * block : (2 * i + k + 1) * block] for i in range(n_block)], axis=1
            )
            hs[k] = half
        hall[slot] = hs[x]
        remote(hs.at[1 - x], hall.at[slot], h_send.at[0], h_recv.at[0], (c, beside))
        remote(hs.at[x], hall.at[slot], h_send.at[1], h_recv.at[1], (other, f))

    def spread():
        theirs = hall.at[(1 - x) * 2 + c]
        wait(theirs, h_recv.at[0])
        remote(theirs, theirs, h_send.at[2], h_recv.at[2], (other, f))

    def attend(part):
        wait(arrived.at[:, :, :, slice(*PARTS[part])], a_recv.at[part])
        half = heads // 2
        for n in range(part * half, (part + 1) * half):
            win, keep = window(n)
            g = rows(gb, win) * keep
            s = dot(rows(qb, win) * keep, rows(kb, win), nt) * scale
            s = jnp.where(same, s, -1e30)
            e = jnp.exp(s - jnp.max(s, axis=1, keepdims=True))
            p = e / jnp.sum(e, axis=1, keepdims=True)
            acc_v[:, win] += dot(p.astype(jnp.bfloat16), g, tn)
            dp = dot(g, rows(vb, win), nt)
            ds = (p * (dp - jnp.sum(p * dp, axis=1, keepdims=True))).astype(jnp.bfloat16)
            acc_q[:, win] += dot(ds, rows(kb, win) * keep, nn)
            acc_k[:, win] += dot(ds, rows(qb, win) * keep, tn)
        cols = slice(*COLS[part])
        grad_v = acc_v[:, cols].astype(jnp.bfloat16)
        out_v[:, :, cols] = grad_v.reshape(N_FRAME, sub, cols.stop - cols.start)
        local(out_v.at[f, :, cols], gall.at[slot, f, :, cols], b_recv.at[part])

        @pl.loop(1, N_FRAME)
        def _(d):
            to = lax.rem(f + d, N_FRAME)
            dst = gall.at[lax.rem(to, 2) * 2 + c, f, :, cols]
            remote(out_v.at[to, :, cols], dst, b_send.at[part], b_recv.at[part], (c, to))

        cat[x, 0, :, cols] = (acc_q[:, cols] * scale).astype(jnp.bfloat16)
        cat[x, 1, :, cols] = (acc_k[:, cols] * scale).astype(jnp.bfloat16)
        cat[x, 2, :, cols] = grad_v

    def swap(part):
        mine = cat.at[x, :, :, slice(*COLS[part])]
        remote(mine, mine, x_sem.at[0, part], x_sem.at[1, part], (c, beside))

    def share(to, core):
        wait(gall.at[0, :, :, slice(*COLS[to])], b_recv.at[to])
        src = gall.at[slot, :, :, slice(*COLS[to])]
        remote(src, src, g_send.at[to], g_recv.at[0 if to == core else 1], (to, beside))
        if to != core:
            remote(src, src, g_send.at[2], g_recv.at[2], (to, f))

    def token_sum(side, cols):
        n = cols.stop - cols.start
        both = pl.ds(side * 2, 2)
        total = dot(
            hall[both].reshape(2 * tok, hall.shape[2]), gall[both, :, :, cols].reshape(2 * tok, n), tn
        )
        return total.reshape(n_block, block, n)

    def weight_here(core):
        cols = slice(*COLS[core])
        wait(hall.at[0], h_recv.at[1])
        wait(gall.at[0, :, :, cols], g_recv.at[2])
        dws[:, :, cols] = token_sum(x, cols)

    def weight(core):
        cols = slice(*COLS[core])
        wait(hall.at[0], h_recv.at[2])
        for i in range(2):
            wait(gall.at[0, :, :, cols], g_recv.at[i])
        dws[:, :, cols] += token_sum(1 - x, cols)
        for zb in range(n_z):
            y_s[zb, :, cols] = dws[zb * 2 + 1 - y, :, cols].astype(jnp.bfloat16)
        remote(y_s.at[:, :, cols], y_r.at[:, :, cols], ry_sem.at[0], ry_sem.at[1], (c, across))

    def sum_y(core):
        cols = slice(*COLS[core])
        wait(y_r.at[:, :, cols], ry_sem.at[1])
        for k in range(1, n_z):
            zb = lax.rem(z + k, n_z)
            total = dws[zb * 2 + y, :, cols] + y_r[zb, :, cols].astype(jnp.float32)
            z_s[zb, :, cols] = total.astype(jnp.bfloat16)
            remote(z_s.at[zb, :, cols], z_r.at[z, :, cols], rz_send, rz_recv, (c, move(f, "z", k)))
        dws[pair, :, cols] += y_r[z, :, cols].astype(jnp.float32)

    def sum_z(core):
        cols = slice(*COLS[core])
        wait(z_r.at[pl.ds(0, n_z - 1), :, cols], rz_recv)
        total = dws[pair, :, cols]
        for k in range(1, n_z):
            total += z_r[lax.rem(z + k, n_z), :, cols].astype(jnp.float32)
        total *= 0.5
        fin_s[:, cols] = total
        remote(fin_s.at[:, cols], fin_r.at[:, cols], f_sem.at[0], f_sem.at[1], (other, f))
        gw_ref[:, cols] = total

    def finish(core):
        mine, rest = slice(*COLS[core]), slice(*COLS[1 - core])
        wait(fin_r.at[:, rest], f_sem.at[1])
        gw_ref[:, rest] = fin_r[:, rest]
        wait(fin_s.at[:, mine], f_sem.at[0])
        wait(y_s.at[:, :, mine], ry_sem.at[0])
        wait(z_s.at[pl.ds(0, n_z - 1), :, mine], rz_send)
        for to in range(2):
            wait(gall.at[0, :, :, slice(*COLS[to])], g_send.at[to])
            if to != core:
                wait(gall.at[0, :, :, slice(*COLS[to])], g_send.at[2])
        w_drain(core)

    def project(j):
        zb = by_distance(j)
        if j == 0:
            for i in range(2):
                wait(cat.at[0, :, :, slice(*COLS[i])], x_sem.at[1, i])
                pltpu.make_async_copy(w_hbm.at[:, slice(*W_COLS[i])], w_part[i].at[pair], loc.at[1 + i]).wait()
        on_core(lambda core: wait(w_part[1 - core].at[pl.ds(0, 2 if j else 1)], wc_recv.at[zb]))
        if j == 0:
            for k in range(2):
                joined[k] = jnp.concatenate([cat[k, i] for i in range(3)], axis=1)
        grads = joined[...].reshape(2 * tok, joined.shape[2])
        parts = [w[pl.ds(zb * 2, 2)].reshape(2 * block, w.shape[2]) for w in w_part]
        res = sum(dot(grads[:, slice(*W_COLS[i])], parts[i], nt) for i in range(2))
        ob[zb] = res.astype(jnp.bfloat16).reshape(2, N_FRAME, sub, 2 * block)
        dst = land.at[x, zb, pl.ds(pair * 2, 2)]
        local(ob.at[zb, :, f], dst, o_recv)

        @pl.loop(1, N_FRAME)
        def _(d):
            to = lax.rem(f + d, N_FRAME)
            remote(ob.at[zb, :, to], dst, o_send, o_recv, (c, to))

    def collect():
        wait(land, o_recv)
        pieces = [
            land[k, zb][:, :, yb * block : (yb + 1) * block].reshape(tok, block)
            for zb in range(n_z) for yb in range(2) for k in range(2)
        ]
        gh_ref[...] = jnp.concatenate(pieces, axis=1)

    steps = {
        "hidden": hidden, "spread": spread, "turn": turn, "plane": plane,
        "collect": collect,
    }
    for i in range(2):
        for h in range(n_z):
            steps["a" + str(i) + str(h)] = functools.partial(exchange, i, h)
        steps["swap" + str(i)] = functools.partial(swap, i)
        steps["attend" + str(i)] = functools.partial(attend, i)
        steps["share" + str(i)] = functools.partial(on_core, functools.partial(share, i))
    for name, fn in (
        ("own_y", w_start_y), ("own_z", w_start_z), ("y0", w_y0), ("ys", w_ys), ("weight", weight), ("weight_here", weight_here), ("sum_y", sum_y),
        ("sum_z", sum_z), ("finish", finish),
    ):
        steps[name] = functools.partial(on_core, fn)
    for i in range(1, n_z):
        steps["hop" + str(i)] = functools.partial(on_core, functools.partial(w_hop, i))
        steps["enter" + str(i)] = functools.partial(enter, i)
        steps["y" + str(i)] = functools.partial(on_core, functools.partial(w_ys, i))
    for j in range(n_z):
        steps["project" + str(j)] = functools.partial(project, j)
    for name in ORDER:
        steps[name]()

    for i in range(2):
        wait(leaving.at[:, pl.ds(0, N_FRAME - 1), :, slice(*PARTS[i])], a_send.at[i])
        wait(out_v.at[pl.ds(0, N_FRAME - 1), :, slice(*COLS[i])], b_send.at[i])
        wait(cat.at[0, :, :, slice(*COLS[i])], x_sem.at[0, i])
    wait(ob.at[:, :, pl.ds(0, N_FRAME - 1)], o_send)
    for i in range(3):
        wait(hs.at[0], h_send.at[i])


def per_device_fused(hidden, queries, keys, values, grad_attn, w_qkv):
    tok, width = hidden.shape[2], hidden.shape[3]
    inner = queries.shape[3]
    block, cat_w = w_qkv.shape
    flat = [
        jnp.swapaxes(a.reshape(tok, inner), 0, 1) for a in (queries, keys, values, grad_attn)
    ]
    bf, f32 = jnp.bfloat16, jnp.float32
    dma = pltpu.SemaphoreType.DMA
    sub, n_block, half = tok // N_FRAME, N_FRAME // 2, width // 2
    n_z = AX["z"][0]
    vmem = pltpu.VMEM
    scratch = (
        [vmem((inner, tok), bf)] * 4
        + [vmem((4, N_FRAME, sub, inner), bf)] * 2
        + [vmem((tok, width), bf), vmem((2, tok, half), bf), vmem((4, tok, half), bf)]
        + [vmem((n_block, block, high - low), bf) for low, high in W_COLS]
        + [vmem((tok, inner), f32)] * 3
        + [vmem((N_FRAME, sub, inner), bf), vmem((4, N_FRAME, sub, inner), bf)]
        + [vmem((2, 3, tok, inner), bf), vmem((2, tok, cat_w), bf)]
        + [vmem((n_z, 2, N_FRAME, sub, 2 * block), bf), vmem((2, n_z, N_FRAME, sub, 2 * block), bf)]
        + [vmem((n_block, block, inner), f32)]
        + [vmem((n_z, block, inner), bf)] * 4
        + [vmem((block, inner), f32)] * 2
        + [dma((3,)), dma((4,)), dma((2,)), dma((2,)), dma((2,)), dma((2,)), dma, dma((n_z, 2)), dma, dma((n_z, 2)), dma, dma((n_z,))]
        + [dma((3,)), dma((3,)), dma((2, 2)), dma((3,)), dma((3,)), dma, dma, dma((2,)), dma, dma, dma((2,))]
        + [pltpu.SemaphoreType.REGULAR, pltpu.SemaphoreType.REGULAR((n_z,))]
    )
    grad_hidden, grad_w = pl.pallas_call(
        kernel,
        out_shape=(
            pltpu.VMEM((tok, width), bf),
            pltpu.VMEM((block, inner), f32),
        ),
        in_specs=[pl.BlockSpec(memory_space=pl.ANY)] * 6,
        out_specs=(pl.BlockSpec(memory_space=pltpu.VMEM),) * 2,
        scratch_shapes=scratch,
        compiler_params=pltpu.CompilerParams(
            collective_id=0, has_side_effects=True, vmem_limit_bytes=60 * 1024 * 1024
        ),
    )(*flat, hidden.reshape(tok, width), w_qkv)
    return grad_hidden.reshape(hidden.shape), grad_w


def solution(mesh):
    in_specs = (
        P("clip", "frame", None, None),
        P("clip", "frame", None, None),
        P("clip", "frame", None, None),
        P("clip", "frame", None, None),
        P("clip", "frame", None, None),
        P("frame", None),
    )
    out_specs = (P("clip", "frame", None, None), P("frame", None))
    fused = mesh.shape["clip"] == 2 and mesh.shape["frame"] == N_FRAME
    return jax.shard_map(
        per_device_fused if fused else per_device, mesh=mesh, in_specs=in_specs, out_specs=out_specs, check_vma=False
    )
```

```python
import functools
import math

import jax
import jax.numpy as jnp
from jax import lax
from jax.experimental import pallas as pl
from jax.experimental.pallas import tpu as pltpu
from jax.sharding import PartitionSpec as P

HDIM = 104


def attend_back(queries, keys, values, grad_out):
    score_scale = 1.0 / math.sqrt(HDIM)
    scores = (
        jnp.einsum("fpnd,gpnd->pnfg", queries, keys, preferred_element_type=jnp.float32)
        * score_scale
    )
    attn_probs = jax.nn.softmax(scores, axis=-1)
    probs_bf = attn_probs.astype(jnp.bfloat16)
    grad_v = jnp.einsum(
        "pnfg,fpnd->gpnd", probs_bf, grad_out, preferred_element_type=jnp.float32
    ).astype(jnp.bfloat16)
    grad_probs = jnp.einsum("fpnd,gpnd->pnfg", grad_out, values, preferred_element_type=jnp.float32)
    grad_scores = attn_probs * (
        grad_probs - jnp.sum(attn_probs * grad_probs, axis=-1, keepdims=True)
    )
    scores_bf = grad_scores.astype(jnp.bfloat16)
    grad_q = (
        jnp.einsum("pnfg,gpnd->fpnd", scores_bf, keys, preferred_element_type=jnp.float32)
        * score_scale
    ).astype(jnp.bfloat16)
    grad_k = (
        jnp.einsum("pnfg,fpnd->gpnd", scores_bf, queries, preferred_element_type=jnp.float32)
        * score_scale
    ).astype(jnp.bfloat16)
    return (grad_q, grad_k, grad_v)


def per_device(hidden, queries, keys, values, grad_attn, w_qkv):
    frames_local = hidden.shape[1]
    patches = hidden.shape[2]
    model_width = hidden.shape[3]
    inner_width = queries.shape[3]
    head_count = inner_width // HDIM
    row_count = frames_local * patches
    head_shape = (frames_local, patches, head_count, HDIM)
    q_local = queries.reshape(head_shape)
    k_local = keys.reshape(head_shape)
    v_local = values.reshape(head_shape)
    g_local = grad_attn.reshape(head_shape)
    q_patch, k_patch, v_patch, g_patch = (
        lax.all_to_all(q_local, "frame", split_axis=1, concat_axis=0, tiled=True),
        lax.all_to_all(k_local, "frame", split_axis=1, concat_axis=0, tiled=True),
        lax.all_to_all(v_local, "frame", split_axis=1, concat_axis=0, tiled=True),
        lax.all_to_all(g_local, "frame", split_axis=1, concat_axis=0, tiled=True),
    )
    grad_q, grad_k, grad_v = attend_back(q_patch, k_patch, v_patch, g_patch)
    grad_q, grad_k, grad_v = (
        lax.all_to_all(grad_q, "frame", split_axis=0, concat_axis=1, tiled=True),
        lax.all_to_all(grad_k, "frame", split_axis=0, concat_axis=1, tiled=True),
        lax.all_to_all(grad_v, "frame", split_axis=0, concat_axis=1, tiled=True),
    )
    value_rows = grad_v.reshape(row_count, inner_width)
    grad_cat = jnp.concatenate(
        [
            grad_q.reshape(row_count, inner_width),
            grad_k.reshape(row_count, inner_width),
            value_rows,
        ],
        axis=1,
    )
    grad_hid = lax.dot_general(
        grad_cat,
        lax.all_gather(w_qkv, "frame", axis=0, tiled=True),
        (((1,), (1,)), ((), ())),
        preferred_element_type=jnp.float32,
    )
    grad_hidden = grad_hid.astype(jnp.bfloat16).reshape(hidden.shape)
    hidden_rows = hidden.reshape(row_count, model_width)
    clip_count = lax.axis_size("clip")
    partial_grad = lax.psum_scatter(
        lax.dot_general(
            hidden_rows, value_rows, (((0,), (0,)), ((), ())), preferred_element_type=jnp.float32
        ),
        "frame",
        scatter_dimension=0,
        tiled=True,
    )
    grad_total = lax.psum(partial_grad, "clip")
    return (grad_hidden, grad_total / clip_count)


AX = {"z": (4, 4), "y": (2, 2), "x": (2, 1)}
N_FRAME = 16
ORDER = (
    "own_y", "own_z", "turn", "plane", "a00", "enter1", "a01", "enter2", "a02", "enter3", "a03",
    "a10", "a11", "a12", "a13", "hop1", "hidden", "spread", "y0", "attend0", "swap0", "attend1", "swap1",
    "hop2", "share0", "share1", "hop3", "y1", "y2", "y3", "weight_here", "weight", "project0", "project1", "project2",
    "project3", "sum_y", "collect", "sum_z", "finish",
)
NEAR = (1, 2, 0, 3)
COLS = ((0, 384), (384, 832))
PARTS = ((0, 512), (512, 832))
W_COLS = ((0, 1152), (1152, 2496))
W_CUT = 384


def move(f, axis, k):
    size, stride = AX[axis]
    digit = lax.rem(lax.div(f, stride), size)
    return f + (lax.rem(digit + k, size) - digit) * stride


def kernel(
    q_hbm, k_hbm, v_hbm, g_hbm, h_hbm, w_hbm,
    gh_ref, gw_ref,
    tq, tk, tv, tg, leaving, arrived,
    hb, hs, hall, w0, w1, acc_q, acc_k, acc_v, out_v, gall, cat, joined, ob, land,
    dws, y_s, y_r, z_s, z_r, fin_s, fin_r,
    loc, t_sem, a_send, a_recv, b_send, b_recv, wy_send, wy_recv, wz_send, wz_recv, wc_send, wc_recv,
    h_send, h_recv, x_sem, g_send, g_recv, o_send, o_recv, ry_sem, rz_send, rz_recv, f_sem, plane_sem, in_sem,
):
    c = lax.axis_index("clip")
    f = lax.axis_index("frame")
    other = 1 - c
    block = w_hbm.shape[0]
    tok = q_hbm.shape[1]
    sub = tok // N_FRAME
    n_block = w0.shape[0]
    n_z = AX["z"][0]
    last = n_z - 1
    scale = 1.0 / math.sqrt(HDIM)
    x = lax.rem(f, 2)
    pair = lax.div(f, 2)
    y = lax.rem(pair, 2)
    z = lax.div(pair, 2)
    beside = f + 1 - 2 * x
    across = move(f, "y", 1)
    slot = x * 2 + c

    def remote(src, dst, ss, rs, peer):
        pltpu.make_async_remote_copy(
            src_ref=src, dst_ref=dst, send_sem=ss, recv_sem=rs,
            device_id=peer, device_id_type=pl.DeviceIdType.MESH,
        ).start()

    def local(src, dst, sem):
        pltpu.make_async_copy(src, dst, sem).start()

    def wait(view, sem):
        pltpu.make_async_copy(view, view, sem).wait()

    def on_core(fn):
        for core in range(2):
            pl.when(c == core)(functools.partial(fn, core))

    barrier = pltpu.get_barrier_semaphore()

    def greet(peer):
        pl.semaphore_signal(barrier, inc=1, device_id=peer, device_id_type=pl.DeviceIdType.MESH)

    for peer in ((c, beside), (c, across), (other, f), (other, beside)):
        greet(peer)
    for way in (1, -1):

        @pl.when((z < last) if way == 1 else (z > 0))
        def _():
            greet((c, f + way * AX["z"][1]))

    turned = ((q_hbm, tq), (k_hbm, tk), (g_hbm, tg), (v_hbm, tv))
    pairs = [(leaving.at[i], arrived.at[i]) for i in range(4)]
    qb, kb, gb, vb = (arrived.at[i] for i in range(4))
    for i, (src, flat) in enumerate(turned):
        local(src, flat, t_sem.at[i])
    local(h_hbm, hb, loc.at[0])
    w_part = (w0, w1)
    for i in range(2):
        local(w_hbm.at[:, slice(*W_COLS[i])], w_part[i].at[pair], loc.at[1 + i])
    pl.semaphore_wait(barrier, 6 - jnp.where((z == 0) | (z == last), 1, 0))

    def tell(sem, peer):
        pl.semaphore_signal(sem, inc=1, device_id=peer, device_id_type=pl.DeviceIdType.MESH)

    def pass_in(from_z, way):
        @pl.when((z < last) if way == 1 else (z > 0))
        def _():
            tell(in_sem.at[from_z], (c, f + way * AX["z"][1]))

    def plane():
        tell(plane_sem, (c, across))
        pl.semaphore_wait(plane_sem, 1)
        for way in (1, -1):
            pass_in(z, way)

    def enter(h):
        for way in (1, -1):
            from_z = z - way * h

            @pl.when((from_z >= 0) & (from_z <= last))
            def _():
                pl.semaphore_wait(in_sem.at[from_z], 1)
                pass_in(from_z, way)

    def cut(core, k):
        return slice(0, W_CUT) if k == 0 else slice(W_CUT, w_part[core].shape[2])

    def w_at(core, zb, yb, k):
        return w_part[core].at[zb * 2 + yb, :, cut(core, k)]

    def w_wait(core, k, sem):
        wait(w_part[core].at[0, :, cut(core, k)], sem)

    def forward(core, zb, yb, k):
        view = w_at(core, zb, yb, k)
        remote(view, view, wc_send, wc_recv.at[zb], (other, f))

    def pass_y(core, zb, k, src=None):
        dst = w_at(core, zb, y, k)
        remote(dst if src is None else src, dst, wy_send, wy_recv.at[zb, k], (c, across))

    def climb(core, zb, way, k, src=None):
        dst = w_at(core, zb, y, k)

        @pl.when((z < last) if way == 1 else (z > 0))
        def _():
            peer = (c, f + way * AX["z"][1])
            remote(dst if src is None else src, dst, wz_send, wz_recv.at[zb, k], peer)

    def own(core, k):
        low, high = W_COLS[core]
        return w_hbm.at[:, (slice(low, low + W_CUT) if k == 0 else slice(low + W_CUT, high))]

    def w_start_y(core):
        for k in range(2):
            pass_y(core, z, k, own(core, k))

    def w_start_z(core):
        for k in range(2):
            for way in (1, -1):
                climb(core, z, way, k, own(core, k))

    def w_hop(h, core):
        for k in range(2):
            for way in (1, -1):
                from_z = z - way * h

                @pl.when((from_z >= 0) & (from_z <= last))
                def _():
                    w_wait(core, k, wz_recv.at[from_z, k])
                    climb(core, from_z, way, k)
                    pass_y(core, from_z, k)
                    forward(core, from_z, y, k)

    def w_y0(core):
        for k in range(2):
            w_wait(core, k, wy_recv.at[z, k])
            forward(core, z, 1 - y, k)

    def by_distance(j):
        at_end = (z == 0) | (z == last)
        up = jnp.where(at_end, j, NEAR[j])
        return jnp.where(z * 2 < n_z, up, last - up)

    def w_ys(j, core):
        zb = by_distance(j)
        for k in range(2):
            w_wait(core, k, wy_recv.at[zb, k])
            forward(core, zb, 1 - y, k)

    def w_drain(core):
        wait(w_part[core].at[pl.ds(0, n_z)], wy_send)
        edge = (z == 0) | (z == last)
        for ends, count in ((True, 1), (False, 5)):

            @pl.when(edge if ends else jnp.logical_not(edge))
            def _():
                wait(w_part[core].at[pl.ds(0, count)], wz_send)

        wait(w_part[core].at[pl.ds(0, n_block - 1)], wc_send)

    def turn():
        for i, (src, _) in enumerate(pairs):
            pltpu.make_async_copy(turned[i][0], turned[i][1], t_sem.at[i]).wait()
            src[...] = turned[i][1][...].T.reshape(src.shape)

    def exchange(part, h):
        cols = slice(*PARTS[part])

        def to_frame(to):
            for src, dst in pairs:
                remote(src.at[to, :, cols], dst.at[f, :, cols], a_send.at[part], a_recv.at[part], (c, to))

        if h == 0:
            for src, dst in pairs:
                local(src.at[f, :, cols], dst.at[f, :, cols], a_recv.at[part])
            for to in (beside, across, move(across, "x", 1)):
                to_frame(to)
            return
        for way in (1, -1):
            to_z = z - way * h

            @pl.when((to_z >= 0) & (to_z <= last))
            def _():
                @pl.loop(0, AX["z"][1])
                def _(k):
                    to_frame(to_z * AX["z"][1] + k)

    acc_q[...] = jnp.zeros_like(acc_q)
    acc_k[...] = jnp.zeros_like(acc_k)
    acc_v[...] = jnp.zeros_like(acc_v)
    row_id = lax.broadcasted_iota(jnp.int32, (tok, tok), 0)
    col_id = lax.broadcasted_iota(jnp.int32, (tok, tok), 1)
    same = lax.rem(row_id, sub) == lax.rem(col_id, sub)

    width_all = q_hbm.shape[0]
    heads = width_all // HDIM
    nt = (((1,), (1,)), ((), ()))
    tn = (((0,), (0,)), ((), ()))
    nn = (((1,), (0,)), ((), ()))
    dot = functools.partial(lax.dot_general, preferred_element_type=jnp.float32)

    def window(n):
        low = n * HDIM // 128 * 128
        high = min(-(-(n + 1) * HDIM // 128) * 128, width_all)
        lane = lax.broadcasted_iota(jnp.int32, (tok, high - low), 1) + low
        keep = jnp.where((lane >= n * HDIM) & (lane < (n + 1) * HDIM), 1.0, 0.0)
        return slice(low, high), keep.astype(jnp.bfloat16)

    def rows(ref, win):
        return ref[:, :, win].reshape(tok, win.stop - win.start)

    def hidden():
        pltpu.make_async_copy(h_hbm, hb, loc.at[0]).wait()
        for k in range(2):
            half = jnp.concatenate(
                [hb[:, (2 * i + k) * block : (2 * i + k + 1) * block] for i in range(n_block)], axis=1
            )
            hs[k] = half
        hall[slot] = hs[x]
        remote(hs.at[1 - x], hall.at[slot], h_send.at[0], h_recv.at[0], (c, beside))
        remote(hs.at[x], hall.at[slot], h_send.at[1], h_recv.at[1], (other, f))

    def spread():
        theirs = hall.at[(1 - x) * 2 + c]
        wait(theirs, h_recv.at[0])
        remote(theirs, theirs, h_send.at[2], h_recv.at[2], (other, f))

    def attend(part):
        wait(arrived.at[:, :, :, slice(*PARTS[part])], a_recv.at[part])
        half = heads // 2
        for n in range(part * half, (part + 1) * half):
            win, keep = window(n)
            g = rows(gb, win) * keep
            s = dot(rows(qb, win) * keep, rows(kb, win), nt) * scale
            s = jnp.where(same, s, -1e30)
            e = jnp.exp(s - jnp.max(s, axis=1, keepdims=True))
            p = e / jnp.sum(e, axis=1, keepdims=True)
            acc_v[:, win] += dot(p.astype(jnp.bfloat16), g, tn)
            dp = dot(g, rows(vb, win), nt)
            ds = (p * (dp - jnp.sum(p * dp, axis=1, keepdims=True))).astype(jnp.bfloat16)
            acc_q[:, win] += dot(ds, rows(kb, win) * keep, nn)
            acc_k[:, win] += dot(ds, rows(qb, win) * keep, tn)
        cols = slice(*COLS[part])
        grad_v = acc_v[:, cols].astype(jnp.bfloat16)
        out_v[:, :, cols] = grad_v.reshape(N_FRAME, sub, cols.stop - cols.start)
        local(out_v.at[f, :, cols], gall.at[slot, f, :, cols], b_recv.at[part])

        @pl.loop(1, N_FRAME)
        def _(d):
            to = lax.rem(f + d, N_FRAME)
            dst = gall.at[lax.rem(to, 2) * 2 + c, f, :, cols]
            remote(out_v.at[to, :, cols], dst, b_send.at[part], b_recv.at[part], (c, to))

        cat[x, 0, :, cols] = (acc_q[:, cols] * scale).astype(jnp.bfloat16)
        cat[x, 1, :, cols] = (acc_k[:, cols] * scale).astype(jnp.bfloat16)
        cat[x, 2, :, cols] = grad_v

    def swap(part):
        mine = cat.at[x, :, :, slice(*COLS[part])]
        remote(mine, mine, x_sem.at[0, part], x_sem.at[1, part], (c, beside))

    def share(to, core):
        wait(gall.at[0, :, :, slice(*COLS[to])], b_recv.at[to])
        src = gall.at[slot, :, :, slice(*COLS[to])]
        remote(src, src, g_send.at[to], g_recv.at[0 if to == core else 1], (to, beside))
        if to != core:
            remote(src, src, g_send.at[2], g_recv.at[2], (to, f))

    def token_sum(side, cols):
        n = cols.stop - cols.start
        both = pl.ds(side * 2, 2)
        total = dot(
            hall[both].reshape(2 * tok, hall.shape[2]), gall[both, :, :, cols].reshape(2 * tok, n), tn
        )
        return total.reshape(n_block, block, n)

    def weight_here(core):
        cols = slice(*COLS[core])
        wait(hall.at[0], h_recv.at[1])
        wait(gall.at[0, :, :, cols], g_recv.at[2])
        dws[:, :, cols] = token_sum(x, cols)

    def weight(core):
        cols = slice(*COLS[core])
        wait(hall.at[0], h_recv.at[2])
        for i in range(2):
            wait(gall.at[0, :, :, cols], g_recv.at[i])
        dws[:, :, cols] += token_sum(1 - x, cols)
        for zb in range(n_z):
            y_s[zb, :, cols] = dws[zb * 2 + 1 - y, :, cols].astype(jnp.bfloat16)
        remote(y_s.at[:, :, cols], y_r.at[:, :, cols], ry_sem.at[0], ry_sem.at[1], (c, across))

    def sum_y(core):
        cols = slice(*COLS[core])
        wait(y_r.at[:, :, cols], ry_sem.at[1])
        for k in range(1, n_z):
            zb = lax.rem(z + k, n_z)
            total = dws[zb * 2 + y, :, cols] + y_r[zb, :, cols].astype(jnp.float32)
            z_s[zb, :, cols] = total.astype(jnp.bfloat16)
            remote(z_s.at[zb, :, cols], z_r.at[z, :, cols], rz_send, rz_recv, (c, move(f, "z", k)))
        dws[pair, :, cols] += y_r[z, :, cols].astype(jnp.float32)

    def sum_z(core):
        cols = slice(*COLS[core])
        wait(z_r.at[pl.ds(0, n_z - 1), :, cols], rz_recv)
        total = dws[pair, :, cols]
        for k in range(1, n_z):
            total += z_r[lax.rem(z + k, n_z), :, cols].astype(jnp.float32)
        total *= 0.5
        fin_s[:, cols] = total
        remote(fin_s.at[:, cols], fin_r.at[:, cols], f_sem.at[0], f_sem.at[1], (other, f))
        gw_ref[:, cols] = total

    def finish(core):
        mine, rest = slice(*COLS[core]), slice(*COLS[1 - core])
        wait(fin_r.at[:, rest], f_sem.at[1])
        gw_ref[:, rest] = fin_r[:, rest]
        wait(fin_s.at[:, mine], f_sem.at[0])
        wait(y_s.at[:, :, mine], ry_sem.at[0])
        wait(z_s.at[pl.ds(0, n_z - 1), :, mine], rz_send)
        for to in range(2):
            wait(gall.at[0, :, :, slice(*COLS[to])], g_send.at[to])
            if to != core:
                wait(gall.at[0, :, :, slice(*COLS[to])], g_send.at[2])
        w_drain(core)

    def project(j):
        zb = by_distance(j)
        if j == 0:
            for i in range(2):
                wait(cat.at[0, :, :, slice(*COLS[i])], x_sem.at[1, i])
                pltpu.make_async_copy(w_hbm.at[:, slice(*W_COLS[i])], w_part[i].at[pair], loc.at[1 + i]).wait()
        on_core(lambda core: wait(w_part[1 - core].at[pl.ds(0, 2 if j else 1)], wc_recv.at[zb]))
        if j == 0:
            for k in range(2):
                joined[k] = jnp.concatenate([cat[k, i] for i in range(3)], axis=1)
        grads = joined[...].reshape(2 * tok, joined.shape[2])
        parts = [w[pl.ds(zb * 2, 2)].reshape(2 * block, w.shape[2]) for w in w_part]
        res = sum(dot(grads[:, slice(*W_COLS[i])], parts[i], nt) for i in range(2))
        ob[zb] = res.astype(jnp.bfloat16).reshape(2, N_FRAME, sub, 2 * block)
        dst = land.at[x, zb, pl.ds(pair * 2, 2)]
        local(ob.at[zb, :, f], dst, o_recv)

        @pl.loop(1, N_FRAME)
        def _(d):
            to = lax.rem(f + d, N_FRAME)
            remote(ob.at[zb, :, to], dst, o_send, o_recv, (c, to))

    def collect():
        wait(land, o_recv)
        pieces = [
            land[k, zb][:, :, yb * block : (yb + 1) * block].reshape(tok, block)
            for zb in range(n_z) for yb in range(2) for k in range(2)
        ]
        gh_ref[...] = jnp.concatenate(pieces, axis=1)

    steps = {
        "hidden": hidden, "spread": spread, "turn": turn, "plane": plane,
        "collect": collect,
    }
    for i in range(2):
        for h in range(n_z):
            steps["a" + str(i) + str(h)] = functools.partial(exchange, i, h)
        steps["swap" + str(i)] = functools.partial(swap, i)
        steps["attend" + str(i)] = functools.partial(attend, i)
        steps["share" + str(i)] = functools.partial(on_core, functools.partial(share, i))
    for name, fn in (
        ("own_y", w_start_y), ("own_z", w_start_z), ("y0", w_y0), ("ys", w_ys), ("weight", weight), ("weight_here", weight_here), ("sum_y", sum_y),
        ("sum_z", sum_z), ("finish", finish),
    ):
        steps[name] = functools.partial(on_core, fn)
    for i in range(1, n_z):
        steps["hop" + str(i)] = functools.partial(on_core, functools.partial(w_hop, i))
        steps["enter" + str(i)] = functools.partial(enter, i)
        steps["y" + str(i)] = functools.partial(on_core, functools.partial(w_ys, i))
    for j in range(n_z):
        steps["project" + str(j)] = functools.partial(project, j)
    for name in ORDER:
        steps[name]()

    for i in range(2):
        wait(leaving.at[:, pl.ds(0, N_FRAME - 1), :, slice(*PARTS[i])], a_send.at[i])
        wait(out_v.at[pl.ds(0, N_FRAME - 1), :, slice(*COLS[i])], b_send.at[i])
        wait(cat.at[0, :, :, slice(*COLS[i])], x_sem.at[0, i])
    wait(ob.at[:, :, pl.ds(0, N_FRAME - 1)], o_send)
    for i in range(3):
        wait(hs.at[0], h_send.at[i])


def per_device_fused(hidden, queries, keys, values, grad_attn, w_qkv):
    tok, width = hidden.shape[2], hidden.shape[3]
    inner = queries.shape[3]
    block, cat_w = w_qkv.shape
    flat = [
        jnp.swapaxes(a.reshape(tok, inner), 0, 1) for a in (queries, keys, values, grad_attn)
    ]
    bf, f32 = jnp.bfloat16, jnp.float32
    dma = pltpu.SemaphoreType.DMA
    sub, n_block, half = tok // N_FRAME, N_FRAME // 2, width // 2
    n_z = AX["z"][0]
    vmem = pltpu.VMEM
    scratch = (
        [vmem((inner, tok), bf)] * 4
        + [vmem((4, N_FRAME, sub, inner), bf)] * 2
        + [vmem((tok, width), bf), vmem((2, tok, half), bf), vmem((4, tok, half), bf)]
        + [vmem((n_block, block, high - low), bf) for low, high in W_COLS]
        + [vmem((tok, inner), f32)] * 3
        + [vmem((N_FRAME, sub, inner), bf), vmem((4, N_FRAME, sub, inner), bf)]
        + [vmem((2, 3, tok, inner), bf), vmem((2, tok, cat_w), bf)]
        + [vmem((n_z, 2, N_FRAME, sub, 2 * block), bf), vmem((2, n_z, N_FRAME, sub, 2 * block), bf)]
        + [vmem((n_block, block, inner), f32)]
        + [vmem((n_z, block, inner), bf)] * 4
        + [vmem((block, inner), f32)] * 2
        + [dma((3,)), dma((4,)), dma((2,)), dma((2,)), dma((2,)), dma((2,)), dma, dma((n_z, 2)), dma, dma((n_z, 2)), dma, dma((n_z,))]
        + [dma((3,)), dma((3,)), dma((2, 2)), dma((3,)), dma((3,)), dma, dma, dma((2,)), dma, dma, dma((2,))]
        + [pltpu.SemaphoreType.REGULAR, pltpu.SemaphoreType.REGULAR((n_z,))]
    )
    grad_hidden, grad_w = pl.pallas_call(
        kernel,
        out_shape=(
            pltpu.VMEM((tok, width), bf),
            pltpu.VMEM((block, inner), f32),
        ),
        in_specs=[pl.BlockSpec(memory_space=pl.ANY)] * 6,
        out_specs=(pl.BlockSpec(memory_space=pltpu.VMEM),) * 2,
        scratch_shapes=scratch,
        compiler_params=pltpu.CompilerParams(
            collective_id=0, has_side_effects=True, vmem_limit_bytes=60 * 1024 * 1024
        ),
    )(*flat, hidden.reshape(tok, width), w_qkv)
    return grad_hidden.reshape(hidden.shape), grad_w


def solution(mesh):
    in_specs = (
        P("clip", "frame", None, None),
        P("clip", "frame", None, None),
        P("clip", "frame", None, None),
        P("clip", "frame", None, None),
        P("clip", "frame", None, None),
        P("frame", None),
    )
    out_specs = (P("clip", "frame", None, None), P("frame", None))
    fused = mesh.shape["clip"] == 2 and mesh.shape["frame"] == N_FRAME
    return jax.shard_map(
        per_device_fused if fused else per_device, mesh=mesh, in_specs=in_specs, out_specs=out_specs, check_vma=False
    )
```
